32 devices in a mesh: rows: 8 (over y, x, core), cols: 4 (over z).
Axes of the slice: x: 2, y: 2, z: 4, core: 2. Of those that a mesh axis runs over, the one named last changes fastest.
Arguments:
- up_a: bfloat16 [28672, 4096], P('rows', 'cols'), may hold values from -6 to 6
- gate_a: bfloat16 [28672, 4096], P('rows', 'cols'), may hold values from -6 to 6
- down_a: bfloat16 [28672, 4096], P('rows', 'cols'), may hold values from -6 to 6
- up_b: bfloat16 [28672, 4096], P('rows', 'cols'), may hold values from -6 to 6
- gate_b: bfloat16 [28672, 4096], P('rows', 'cols'), may hold values from -6 to 6
- down_b: bfloat16 [28672, 4096], P('rows', 'cols'), may hold values from -6 to 6
- perm: int32 [28672], P('rows'), may hold values from 0 to 28671, as said below
Outputs:
- costs: float32 [28672, 256], P('rows', 'cols')
- up_mean: bfloat16 [28672, 4096], P('rows', 'cols')
- gate_mean: bfloat16 [28672, 4096], P('rows', 'cols')
- down_mean: bfloat16 [28672, 4096], P('rows', 'cols')
The draws below stay inside these ranges and needn't reach their ends.
Inputs may be any that keep to these rules, and one draw needn't show every extreme that they name: perm is a permutation of the hidden units. Split positions and values alike into aligned blocks of 3584: the positions of one block take at most 448 values from any one block, and exactly 448 from some block.
All inputs are finite; a program needn't handle non-finite values.
Results may differ from the reference program's by a relative error of at most 0.001.
Values may be sent and summed in bfloat16 or wider, within the bound.
A program may use at most 192 MiB of HBM per device.

```python
import jax
import jax.numpy as jnp
from jax import lax

D = 4096
FF = 28672
BLOCKS = 8
FF_DEV = 3584
WIN = 256
STRIDE = 112
CAP = 448
N_ROWS = 8


def draw_perm(key, part):
    peers = N_ROWS
    row_count = FF_DEV
    capacity = CAP
    key_offset, key_rest, key_rows, key_order = jax.random.split(key, 4)
    offset_dev = jax.random.randint(key_offset, (), 0, peers).astype(jnp.int32)
    spare_rows = row_count - capacity
    rounds = max(1, (spare_rows + peers - 2) // (peers - 1))
    round_keys = jax.random.split(key_rest, rounds)
    others = jax.vmap(lambda one_key: jax.random.permutation(one_key, peers - 1))(round_keys)
    others = others.reshape(-1)[:spare_rows].astype(jnp.int32)
    shifts = jnp.concatenate([jnp.full((capacity,), 0, jnp.int32) + offset_dev, (offset_dev + 1 + others) % peers])
    local_rows = jax.random.permutation(key_rows, row_count).astype(jnp.int32)
    order_keys = jax.random.split(key_order, peers)
    orders = jax.vmap(lambda one_key: jax.random.permutation(one_key, row_count))(order_keys).astype(jnp.int32)
    blocks = jnp.arange(peers, dtype=jnp.int32)[:, None]
    source = (blocks + shifts[orders]) % peers
    return (source * row_count + local_rows[orders]).reshape(-1).astype(jnp.int32)


def shard_levels(key, shape, cuts, smallest, largest):
    level, own = 1.0, jax.random.fold_in(key, 6)
    for axis_at, shards_of in cuts:
        draws = jnp.exp(jax.random.uniform(jax.random.fold_in(own, axis_at), (shards_of,), jnp.float32, smallest / len(cuts), largest / len(cuts)))
        level = level * jnp.repeat(draws, shape[axis_at] // shards_of).reshape([-1 if axis == axis_at else 1 for axis in range(len(shape))])
    return level


def normal_values(rng, dims, spread, reach, cuts=(), kind=jnp.bfloat16):
    array = jax.random.normal(rng, dims, jnp.float32) * spread
    if len(cuts) > 0:
        array = shard_levels(rng, dims, cuts, -0.22, 0.18) * array
    return jnp.clip(array, min=-reach, max=reach).astype(kind)


def setup_inputs(seed: int = 0) -> dict:
    streams_of = jax.random.split(jax.random.key(seed), 8)
    up_a = normal_values(streams_of[0], (FF, D), 1.0, 6.0, ((0, 8), (1, 4)))
    gate_a = normal_values(streams_of[1], (FF, D), 1.0, 6.0, ((0, 8), (1, 4)))
    down_a = normal_values(streams_of[2], (FF, D), 1.0, 6.0, ((0, 8), (1, 4)))
    up_b = normal_values(streams_of[3], (FF, D), 1.0, 6.0, ((0, 8), (1, 4)))
    gate_b = normal_values(streams_of[4], (FF, D), 1.0, 6.0, ((0, 8), (1, 4)))
    down_b = normal_values(streams_of[5], (FF, D), 1.0, 6.0, ((0, 8), (1, 4)))
    perm = draw_perm(jax.random.fold_in(streams_of[7], 71), 0)
    return dict(up_a=up_a, gate_a=gate_a, down_a=down_a, up_b=up_b, gate_b=gate_b, down_b=down_b, perm=perm)


def reference(up_a, gate_a, down_a, up_b, gate_b, down_b, perm):
    columns = jnp.arange(WIN, dtype=jnp.int32)
    window_neurons = (columns % BLOCKS) * FF_DEV + (columns // BLOCKS) * STRIDE
    window_up = up_a[window_neurons].astype(jnp.float32)
    window_gate = gate_a[window_neurons].astype(jnp.float32)
    cost_scale = (2.0 * D) ** -0.5
    costs = jnp.dot(up_b.astype(jnp.float32), window_up.T, precision=lax.Precision.HIGHEST)
    costs = costs + jnp.dot(gate_b.astype(jnp.float32), window_gate.T, precision=lax.Precision.HIGHEST)
    costs = costs * cost_scale
    results = []
    for initial, other in ((up_a, up_b), (gate_a, gate_b), (down_a, down_b)):
        matched = other[perm].astype(jnp.float32)
        results.append(((initial.astype(jnp.float32) + matched) * 0.5).astype(jnp.bfloat16))
    return (costs, results[0], results[1], results[2])
```

```python
import functools

import jax
import jax.numpy as jnp
from jax import lax
from jax.experimental import pallas as pl
from jax.experimental.pallas import tpu as pltpu
from jax.sharding import PartitionSpec as P

D = 4096
A_DEV = 32
MESH = pl.DeviceIdType.MESH

PEERS = 8
LANES = 128
TILE = 256
SLOT = 64
CODE = 1024


def one_hot(hit):
    return jnp.where(hit, 1.0, 0.0).astype(jnp.bfloat16)


def matmul(a, b):
    return jnp.dot(a, b, preferred_element_type=jnp.float32)


def ask_kernel(count, perm_ref, asked_ref, code_ref, before_ref, hot, halves, counts, sent, got, send_sems, recv_sems, own_sem):
    me = lax.axis_index("rows")
    barrier = pltpu.get_barrier_semaphore()
    for k in range(1, PEERS):
        pl.semaphore_signal(barrier, inc=1, device_id={"rows": me ^ k}, device_id_type=MESH)

    pad = perm_ref.shape[0]
    used = count // LANES
    slots = count // PEERS
    perm = perm_ref[...]
    source = jnp.zeros_like(perm)
    for k in range(1, PEERS + 1):
        source = source + jnp.where(perm >= k * count, 1, 0)
    row = perm - source * count
    masks = jnp.concatenate([jnp.where(source == k, 1.0, 0.0) for k in range(PEERS)], axis=0)
    packed = masks.astype(jnp.bfloat16)
    shape = (LANES, LANES)
    lane_before = one_hot(lax.broadcasted_iota(jnp.int32, shape, 0) < lax.broadcasted_iota(jnp.int32, shape, 1))
    within = matmul(packed, lane_before)
    totals = matmul(packed, jnp.ones(shape, jnp.bfloat16)).astype(jnp.bfloat16)
    shape = (PEERS * pad, PEERS * pad)
    left, right = lax.broadcasted_iota(jnp.int32, shape, 0), lax.broadcasted_iota(jnp.int32, shape, 1)
    row_before = one_hot((right < left) & (right >= left - lax.rem(left, pad)))
    ahead = matmul(row_before, totals)
    counts[...] = ahead.astype(jnp.int32)
    ranked = masks * (within + ahead)
    rank = ranked[:pad]
    for k in range(1, PEERS):
        rank = rank + ranked[k * pad : (k + 1) * pad]
    rank = rank.astype(jnp.int32)
    code_ref[...] = (source ^ me) * CODE + rank
    for k in range(PEERS):
        before_ref[k] = counts[pl.ds(pl.multiple_of((me ^ k) * pad, pad), pad), :]

    high = lax.shift_right_logical(row, 8).astype(jnp.float32)
    low = (row & 255).astype(jnp.float32)
    block = lax.broadcasted_iota(jnp.int32, (PEERS, LANES), 0)
    slot = lax.broadcasted_iota(jnp.int32, (slots, LANES), 0)
    for j in range(used):
        at = slice(j * LANES, (j + 1) * LANES)
        one = slice(j, j + 1)
        mine = source[one] == block
        both = [jnp.where(mine, part[one], 0.0) for part in (high, low)]
        halves[:, at] = jnp.concatenate(both, axis=0).astype(jnp.bfloat16)
        hot[:, at] = one_hot(rank[one] == slot)
    found = lax.dot_general(halves[...], hot[...], (((1,), (1,)), ((), ())), preferred_element_type=jnp.float32)
    wanted = found[:PEERS] * 256.0 + found[PEERS:]
    for k in range(PEERS):
        sent[k, :, :slots] = jnp.broadcast_to(wanted[k : k + 1], (8, slots))
        sent[k, :, slots:] = jnp.zeros((8, sent.shape[2] - slots), jnp.float32)

    pl.semaphore_wait(barrier, PEERS - 1)
    copies = []
    for k in range(1, PEERS):
        peer = me ^ k
        copy = pltpu.make_async_remote_copy(
            src_ref=sent.at[peer],
            dst_ref=got.at[k],
            send_sem=send_sems.at[k],
            recv_sem=recv_sems.at[k],
            device_id={"rows": peer},
            device_id_type=MESH,
        )
        copy.start()
        copies.append(copy)
    own = pltpu.make_async_copy(sent.at[me], got.at[0], own_sem)
    own.start()
    own.wait()
    for copy in copies:
        copy.wait()
    table = jnp.concatenate([got[k, 0:1, :] for k in range(PEERS)], axis=0)
    table = jnp.concatenate([table] * (LANES // PEERS), axis=0)
    asked_ref[...] = table.T.astype(jnp.int32)


def ask(perm):
    count = perm.shape[0]
    used = count // LANES
    pad = -(-used // 8) * 8
    slots = count // PEERS
    wide = -(-slots // LANES) * LANES
    grid = jnp.pad(perm.reshape(used, LANES), ((0, pad - used), (0, 0)), constant_values=PEERS * count)
    vmem = pl.BlockSpec(memory_space=pltpu.VMEM)
    return pl.pallas_call(
        functools.partial(ask_kernel, count),
        out_shape=(
            jax.ShapeDtypeStruct((wide, LANES), jnp.int32),
            jax.ShapeDtypeStruct((pad, LANES), jnp.int32),
            jax.ShapeDtypeStruct((PEERS, pad, LANES), jnp.int32),
        ),
        in_specs=[vmem],
        out_specs=(vmem,) * 3,
        scratch_shapes=[
            pltpu.VMEM((slots, count), jnp.bfloat16),
            pltpu.VMEM((2 * PEERS, count), jnp.bfloat16),
            pltpu.VMEM((PEERS * pad, LANES), jnp.int32),
            pltpu.VMEM((PEERS, 8, wide), jnp.float32),
            pltpu.VMEM((PEERS, 8, wide), jnp.float32),
            pltpu.SemaphoreType.DMA((PEERS,)),
            pltpu.SemaphoreType.DMA((PEERS,)),
            pltpu.SemaphoreType.DMA,
        ],
        compiler_params=pltpu.CompilerParams(
            collective_id=0, has_side_effects=True, vmem_limit_bytes=32 * 1024 * 1024
        ),
    )(grid)


def window_kernel(stride, up_ref, gate_ref, out_ref, held, sems):
    copies = []
    for m, ref in enumerate((up_ref, gate_ref)):
        for i in range(A_DEV):
            at = m * A_DEV + i
            copy = pltpu.make_async_copy(ref.at[pl.ds(i * stride, 16)], held.at[pl.ds(at * 16, 16)], sems.at[at])
            copy.start()
            copies.append(copy)
    for copy in copies:
        copy.wait()
    shape = (2 * A_DEV, 32 * A_DEV)
    first = lax.broadcasted_iota(jnp.int32, shape, 0) * 16 == lax.broadcasted_iota(jnp.int32, shape, 1)
    out_ref[...] = matmul(one_hot(first), held[...]).astype(jnp.bfloat16)


def window_units(up_a, gate_a):
    features = up_a.shape[1]
    whole = pl.BlockSpec(memory_space=pl.ANY)
    return pl.pallas_call(
        functools.partial(window_kernel, up_a.shape[0] // A_DEV),
        out_shape=jax.ShapeDtypeStruct((2 * A_DEV, features), jnp.bfloat16),
        in_specs=[whole, whole],
        out_specs=pl.BlockSpec(memory_space=pltpu.VMEM),
        scratch_shapes=[
            pltpu.VMEM((32 * A_DEV, features), jnp.bfloat16),
            pltpu.SemaphoreType.DMA((2 * A_DEV,)),
        ],
    )(up_a, gate_a)


def collect_kernel(shifts, asked_ref, rows_ref, *refs):
    outs, total = refs[: len(shifts)], refs[-1]
    step = pl.program_id(1)
    depth = rows_ref.shape[0]
    slots = outs[0].shape[0]
    row = lax.broadcasted_iota(jnp.int32, (slots, depth), 1) + step * depth
    hot = jnp.concatenate([one_hot(asked_ref[:slots, k : k + 1] == row) for k in shifts], axis=0)
    part = matmul(hot, rows_ref[...])

    @pl.when(step == 0)
    def _():
        total[...] = part

    @pl.when(step > 0)
    def _():
        total[...] += part

    @pl.when(step == pl.num_programs(1) - 1)
    def _():
        for at, out in enumerate(outs):
            out[...] = total[at * slots : (at + 1) * slots].astype(out.dtype)


def collect(asked, rows, shifts, start, size):
    count = rows.shape[0]
    slots = count // PEERS
    depth = 512 if count % 512 == 0 else slots
    n = len(shifts)
    return pl.pallas_call(
        functools.partial(collect_kernel, shifts),
        out_shape=[jax.ShapeDtypeStruct((slots, size), rows.dtype)] * n,
        grid=(1, count // depth),
        in_specs=[
            pl.BlockSpec(asked.shape, lambda c, s: (0, 0)),
            pl.BlockSpec((depth, size), lambda c, s: (s, start // size)),
        ],
        out_specs=[pl.BlockSpec((slots, size), lambda c, s: (0, 0))] * n,
        scratch_shapes=[pltpu.VMEM((n * slots, size), jnp.float32)],
        compiler_params=pltpu.CompilerParams(vmem_limit_bytes=60 * 1024 * 1024),
        cost_estimate=pl.CostEstimate(
            flops=2 * n * slots * count * size, bytes_accessed=2 * (count + n * slots) * size, transcendentals=0
        ),
    )(asked, rows)


def place_kernel(before_ref, code_ref, initial_ref, *refs):
    *rest, out_ref, held, total = refs
    arrived = rest[-PEERS:]
    t = pl.program_id(0)
    pad = before_ref.shape[0] // PEERS
    last = arrived[0].shape[0] - SLOT
    per = TILE // LANES
    starts, rounds = [], jnp.int32(1)
    for k in range(PEERS):
        lo = before_ref[k * pad + t * per]
        hi = before_ref[k * pad + t * per + per]
        start = lax.shift_left(lax.shift_right_logical(lo, 4), 4)
        starts.append(start)
        rounds = jnp.maximum(rounds, lax.shift_right_logical(hi - start + SLOT - 1, 6))
    lane = lax.broadcasted_iota(jnp.int32, (1, PEERS * SLOT), 1)
    peer = lax.shift_right_logical(lane, 6)
    code = code_ref[...]
    code = code[:, :1]

    def gathered(j):
        first = jnp.zeros_like(lane)
        at = jnp.zeros_like(lane)
        for k in range(PEERS):
            begin = starts[k] + j * SLOT
            from_row = jnp.minimum(begin, last)
            held[k * SLOT : (k + 1) * SLOT, :] = arrived[k][pl.ds(pl.multiple_of(from_row, 16), SLOT), :]
            first = jnp.where(peer == k, begin, first)
            at = jnp.where(peer == k, from_row, at)
        at = at + (lane & (SLOT - 1))
        codes = jnp.where(at >= first, peer * CODE + at, -1)
        return matmul(one_hot(code == codes), held[...])

    total[...] = gathered(jnp.int32(0))

    def more(j, carry):
        total[...] += gathered(j)
        return carry

    lax.fori_loop(1, rounds, more, 0)
    out_ref[...] = ((initial_ref[...].astype(jnp.float32) + total[...]) * 0.5).astype(out_ref.dtype)


def place(before, code, initial, arrived, start, out=None):
    count, features = initial.shape
    slots, size = arrived[0].shape
    wide = lambda t, *_: (t, start // size)
    extra = [] if out is None else [out]
    return pl.pallas_call(
        place_kernel,
        out_shape=jax.ShapeDtypeStruct((count, features), initial.dtype),
        grid_spec=pltpu.PrefetchScalarGridSpec(
            num_scalar_prefetch=1,
            grid=(count // TILE,),
            in_specs=[
                pl.BlockSpec((TILE, LANES), lambda t, *_: (t, 0)),
                pl.BlockSpec((TILE, size), wide),
            ]
            + [pl.BlockSpec(memory_space=pl.ANY)] * len(extra)
            + [pl.BlockSpec((slots, size), lambda t, *_: (0, 0))] * PEERS,
            out_specs=pl.BlockSpec((TILE, size), wide),
            scratch_shapes=[
                pltpu.VMEM((PEERS * SLOT, size), jnp.bfloat16),
                pltpu.VMEM((TILE, size), jnp.float32),
            ],
        ),
        input_output_aliases={3: 0} if extra else {},
        compiler_params=pltpu.CompilerParams(vmem_limit_bytes=60 * 1024 * 1024),
        cost_estimate=pl.CostEstimate(
            flops=2 * count * PEERS * SLOT * size, bytes_accessed=6 * count * size, transcendentals=0
        ),
    )(before, code, initial, *extra, *arrived)


def balanced(up_a, gate_a, down_a, up_b, gate_b, down_b, perm):
    row_count, features = up_a.shape
    cols = lax.axis_size("cols")
    cost_scale = (2.0 * D) ** (-0.5)

    window = window_units(up_a, gate_a)
    perm, window = lax.optimization_barrier((perm, window))
    pieces = lax.all_gather(window, "rows")
    asked, code, before = ask(perm)
    before = before[:, :, 0].reshape(-1)
    code = jnp.broadcast_to(code.reshape(-1)[:row_count, None], (row_count, LANES))

    def after(value, *others):
        return lax.optimization_barrier((value,) + others)[0]

    def send(rows, start, size, group, *others):
        parts = collect(after(asked, *others), rows, group, start, size)
        return parts, {
            k: part if k == 0 else lax.ppermute(part, "rows", [(i, i ^ k) for i in range(PEERS)])
            for k, part in zip(group, parts)
        }

    def placed(initial, arrived, start, out, *others):
        return place(before, after(code, *others), initial, [arrived[k] for k in range(PEERS)], start, out)

    near, far, every = (6, 2, 4), (7, 3, 5, 1, 0), (6, 2, 4, 7, 3, 5, 1, 0)
    half, quarter = features // 2, features // 4
    parts, up_first = send(up_b, 0, features, near[:1])
    parts, up_second = send(up_b, 0, features, near[1:], *parts)
    up_first = {**up_first, **up_second}
    parts, up_last = send(up_b, 0, features, far, *parts)

    pieces = after(pieces, *parts)
    wide = pieces.reshape(PEERS, 2, A_DEV, features).transpose(1, 2, 0, 3).reshape(2, A_DEV * PEERS, features)
    partial_value = jnp.einsum("kd,jd->kj", wide[0], up_b, preferred_element_type=jnp.float32)
    partial_value = partial_value + jnp.einsum("kd,jd->kj", wide[1], gate_b, preferred_element_type=jnp.float32)
    total = lax.psum_scatter(partial_value.reshape(cols, -1, row_count), "cols", scatter_dimension=0)

    parts, gate_first = send(gate_b, 0, features, near, partial_value, *up_first.values())
    parts, gate_last = send(gate_b, 0, features, far, *parts, *up_last.values())
    up_mean = placed(up_a, {**up_first, **up_last}, 0, None, *parts)
    parts, down_first = send(down_b, 0, half, near, up_mean, *gate_first.values())
    parts, down_second = send(down_b, 0, half, far, *parts, *gate_last.values())
    gate_mean = placed(gate_a, {**gate_first, **gate_last}, 0, None, *parts)
    parts, down_third = send(down_b, half, quarter, every, gate_mean, *down_first.values())
    parts, down_fourth = send(down_b, half + quarter, quarter, every, *parts, *down_second.values())
    down_mean = placed(down_a, {**down_first, **down_second}, 0, None, *parts)
    down_mean = placed(down_a, down_third, half, down_mean)
    costs = (after(total, down_mean) * cost_scale).T
    down_mean = placed(down_a, down_fourth, half + quarter, down_mean, costs)
    return (costs, up_mean, gate_mean, down_mean)


def pick(array, index):
    rows = jnp.arange(array.shape[0], dtype=jnp.int32)
    hot = (index[:, None] == rows[None, :]).astype(array.dtype)
    return jnp.dot(hot, array, preferred_element_type=jnp.float32).astype(array.dtype)


def mix(initial, picked):
    return ((initial.astype(jnp.float32) + picked.astype(jnp.float32)) * 0.5).astype(jnp.bfloat16)


def general(up_a, gate_a, down_a, up_b, gate_b, down_b, perm):
    row_count, features = up_a.shape
    stride = row_count // A_DEV
    cost_scale = (2.0 * D) ** (-0.5)
    peers = lax.axis_size("rows")
    cols = lax.axis_size("cols")
    capacity = max(2, (row_count + peers - 1) // peers)

    source = perm // row_count
    local_row = perm % row_count
    blocks = jnp.arange(peers, dtype=jnp.int32)
    matches = (source[None, :] == blocks[:, None]).astype(jnp.int32)
    order = jnp.arange(row_count, dtype=jnp.int32)
    ahead = jnp.dot(
        matches.astype(jnp.bfloat16),
        (order[:, None] < order[None, :]).astype(jnp.bfloat16),
        preferred_element_type=jnp.float32,
    )
    arrival_rank = jnp.sum(ahead.astype(jnp.int32) * matches, axis=0)
    high = (local_row // 256).astype(jnp.bfloat16)
    low = (local_row % 256).astype(jnp.bfloat16)
    halves = jnp.stack([high, low])[:, None, :] * matches.astype(jnp.bfloat16)[None]
    at_rank = (arrival_rank[None, :] == jnp.arange(capacity, dtype=jnp.int32)[:, None]).astype(jnp.bfloat16)
    found = jnp.einsum("hsi,ri->hsr", halves, at_rank, preferred_element_type=jnp.float32)
    wanted = found[0].astype(jnp.int32) * 256 + found[1].astype(jnp.int32)
    asked = lax.all_to_all(wanted, "rows", split_axis=0, concat_axis=0, tiled=True).reshape(-1)
    slot = source * capacity + arrival_rank

    window = jnp.concatenate([up_a[::stride], gate_a[::stride]], axis=0)
    pieces = lax.all_gather(window, "rows").reshape(peers, 2, A_DEV, features)
    wide = pieces.transpose(1, 2, 0, 3).reshape(2, A_DEV * peers, features)
    partial_value = jnp.einsum("kd,jd->kj", wide[0], up_b, preferred_element_type=jnp.float32)
    partial_value = partial_value + jnp.einsum("kd,jd->kj", wide[1], gate_b, preferred_element_type=jnp.float32)
    total = lax.psum_scatter(partial_value.reshape(cols, -1, row_count), "cols", scatter_dimension=0)

    def averaged(initial, other):
        moved = pick(other, asked).reshape(peers, capacity, features)
        moved = lax.all_to_all(moved, "rows", split_axis=0, concat_axis=0, tiled=True)
        return mix(initial, pick(moved.reshape(-1, features), slot))

    return (
        (total * cost_scale).T,
        averaged(up_a, up_b),
        averaged(gate_a, gate_b),
        averaged(down_a, down_b),
    )


def solution(mesh):
    def local(up_a, *rest):
        row_count, features = up_a.shape
        even = mesh.shape["rows"] == PEERS and row_count % (PEERS * 16) == 0 and row_count % (A_DEV * 16) == 0
        even = even and row_count % TILE == 0 and SLOT <= row_count // PEERS < CODE and features % 512 == 0
        return (balanced if even else general)(up_a, *rest)

    placed = (P("rows", "cols"),) * 6 + (P("rows"),)
    return jax.shard_map(
        local,
        mesh=mesh,
        in_specs=placed,
        out_specs=(P("rows", "cols"),) * 4,
        check_vma=False,
    )
```

```python
import functools

import jax
import jax.numpy as jnp
from jax import lax
from jax.experimental import pallas as pl
from jax.experimental.pallas import tpu as pltpu
from jax.sharding import PartitionSpec as P

D = 4096
A_DEV = 32
MESH = pl.DeviceIdType.MESH

PEERS = 8
LANES = 128
TILE = 256
SLOT = 64
COST_ROWS = 512
OVER_LANES = (((1,), (1,)), ((), ()))
CODE = 1024


def one_hot(hit):
    return jnp.where(hit, 1.0, 0.0).astype(jnp.bfloat16)


def matmul(a, b):
    return jnp.dot(a, b, preferred_element_type=jnp.float32)


def count_ranks(count, me, perm_ref, code_ref, slot_ref, before_ref, hot, halves, counts, sent):
    pad = perm_ref.shape[0]
    used = count // LANES
    slots = count // PEERS
    perm = perm_ref[...]
    source = jnp.zeros_like(perm)
    for k in range(1, PEERS + 1):
        source = source + jnp.where(perm >= k * count, 1, 0)
    row = perm - source * count
    masks = jnp.concatenate([jnp.where(source == k, 1.0, 0.0) for k in range(PEERS)], axis=0)
    packed = masks.astype(jnp.bfloat16)
    shape = (LANES, LANES)
    lane_before = one_hot(lax.broadcasted_iota(jnp.int32, shape, 0) < lax.broadcasted_iota(jnp.int32, shape, 1))
    within = matmul(packed, lane_before)
    totals = matmul(packed, jnp.ones(shape, jnp.bfloat16)).astype(jnp.bfloat16)
    shape = (PEERS * pad, PEERS * pad)
    left, right = lax.broadcasted_iota(jnp.int32, shape, 0), lax.broadcasted_iota(jnp.int32, shape, 1)
    row_before = one_hot((right < left) & (right >= left - lax.rem(left, pad)))
    ahead = matmul(row_before, totals)
    counts[...] = ahead.astype(jnp.int32)
    ranked = masks * (within + ahead)
    rank = ranked[:pad]
    for k in range(1, PEERS):
        rank = rank + ranked[k * pad : (k + 1) * pad]
    rank = rank.astype(jnp.int32)
    code_ref[...] = (source ^ me) * CODE + rank
    slot_ref[...] = jnp.minimum((source ^ me) * slots + rank, count - 1)
    for k in range(PEERS):
        before_ref[k] = counts[pl.ds(pl.multiple_of((me ^ k) * pad, pad), pad), :]

    high = lax.shift_right_logical(row, 8).astype(jnp.float32)
    low = (row & 255).astype(jnp.float32)
    block = lax.broadcasted_iota(jnp.int32, (PEERS, LANES), 0)
    slot = lax.broadcasted_iota(jnp.int32, (slots, LANES), 0)
    for j in range(used):
        at = slice(j * LANES, (j + 1) * LANES)
        one = slice(j, j + 1)
        mine = source[one] == block
        both = [jnp.where(mine, part[one], 0.0) for part in (high, low)]
        halves[:, at] = jnp.concatenate(both, axis=0).astype(jnp.bfloat16)
        hot[:, at] = one_hot(rank[one] == slot)
    found = lax.dot_general(halves[...], hot[...], OVER_LANES, preferred_element_type=jnp.float32)
    wanted = found[:PEERS] * 256.0 + found[PEERS:]
    for k in range(PEERS):
        sent[k, :, :slots] = jnp.broadcast_to(wanted[k : k + 1], (8, slots)).astype(jnp.int32)
        sent[k, :, slots:] = jnp.zeros((8, sent.shape[2] - slots), jnp.int32)


def spread_out(rows_ref, spread, base=0):
    tall, width = rows_ref.shape
    tiles = width // LANES

    def step(m, carry):
        for c in range(tiles):
            v = rows_ref[pl.ds(pl.multiple_of(m * 16, 16), 16), c * LANES : (c + 1) * LANES].astype(jnp.float32)
            for h in range(2):
                to = base + (m * 2 + h) * 8 * tiles + c * 8
                spread[pl.ds(pl.multiple_of(to, 8), 8), :] = v[h * 8 : h * 8 + 8]
        return carry

    lax.fori_loop(0, tall // 16, step, 0)


def sixteen(index_of, spread, turn, tiles):
    for s in range(16):
        i = index_of(s)
        begin = lax.shift_right_logical(i, 3) * (8 * tiles) + (i & 7)
        turn[pl.ds((s // 8) * 8 * tiles + s % 8, tiles, stride=8), :] = spread[pl.ds(begin, tiles, stride=8), :]
    for c in range(tiles):
        yield c, jnp.concatenate([turn[(h * tiles + c) * 8 : (h * tiles + c + 1) * 8, :] for h in range(2)], axis=0)


def first_kernel(count, chunks, perm_ref, up_a, gate_a, up_b, gate_b, down_b, code_ref, slot_ref, before_ref, partial_ref, up_moved, up_sent, *refs):
    gate_rows, refs = refs[:PEERS], refs[PEERS:]
    down_rows = [refs[n * PEERS : (n + 1) * PEERS] for n in range(len(chunks))]
    refs = refs[len(chunks) * PEERS :]
    hot, halves, counts, sent, got, asked, held, window, windows, wide, rows, spread, turn, stage, part = refs[:15]
    ask_send, ask_recv, up_send, up_recv, win_send, win_recv, strip_sems, load_sems, stage_sems, own_sem, part_sem = refs[15:]
    me = lax.axis_index("rows")
    slots = count // PEERS
    stride = count // A_DEV
    barrier = pltpu.get_barrier_semaphore()
    for k in range(1, PEERS):
        pl.semaphore_signal(barrier, inc=1, device_id={"rows": me ^ k}, device_id_type=MESH)

    strips = []
    for m, ref in enumerate((up_a, gate_a)):
        for i in range(A_DEV):
            at = m * A_DEV + i
            strips.append(
                pltpu.make_async_copy(ref.at[pl.ds(i * stride, 16)], held.at[pl.ds(at * 16, 16)], strip_sems.at[at])
            )
    for copy in strips:
        copy.start()
    loads = [pltpu.make_async_copy(ref, rows.at[n], load_sems.at[n]) for n, ref in enumerate((up_b, gate_b))]
    for copy in loads:
        copy.start()

    for copy in strips:
        copy.wait()
    shape = (2 * A_DEV, 32 * A_DEV)
    first = lax.broadcasted_iota(jnp.int32, shape, 0) * 16 == lax.broadcasted_iota(jnp.int32, shape, 1)
    window[...] = matmul(one_hot(first), held[...]).astype(jnp.bfloat16)
    windows[0] = window[...]
    pl.semaphore_wait(barrier, PEERS - 1)

    def remote(src, dst, send, recv, peer):
        return pltpu.make_async_remote_copy(
            src_ref=src, dst_ref=dst, send_sem=send, recv_sem=recv, device_id={"rows": peer}, device_id_type=MESH
        )

    across = [
        remote(window, windows.at[k], win_send.at[k], win_recv.at[k], me ^ k) for k in (6, 2, 4)
    ]
    for copy in across:
        copy.start()

    count_ranks(count, me, perm_ref, code_ref, slot_ref, before_ref, hot, halves, counts, sent)
    asks = [remote(sent.at[me ^ k], got.at[k], ask_send.at[k], ask_recv.at[k], me ^ k) for k in (6, 7, 4, 5, 2, 3, 1)]
    for copy in asks:
        copy.start()
    own = pltpu.make_async_copy(sent.at[me], got.at[0], own_sem)
    own.start()
    loads[0].wait()
    spread_out(rows.at[0], spread)
    own.wait()
    for copy in asks:
        copy.wait()
    got[...] = jnp.clip(got[...], 0, count - 1)
    own = pltpu.make_async_copy(got, asked, own_sem)
    own.start()
    own.wait()

    def gather(k, buffer):
        def step(t, carry):
            for c, tile in sixteen(lambda s: asked[k, 0, t * 16 + s], spread, turn, 8):
                stage[buffer, pl.ds(pl.multiple_of(t * 16, 16), 16), c * LANES : (c + 1) * LANES] = tile.astype(
                    jnp.bfloat16
                )
            return carry

        lax.fori_loop(0, slots // 16, step, 0)

    def up_step(n, carry):
        k = n ^ 6
        gather(k, 0)

        @pl.when(k > 0)
        def _():
            copy = pltpu.make_async_copy(stage.at[0], up_sent.at[k], stage_sems.at[0])
            copy.start()
            copy.wait()
            remote(up_sent.at[k], up_moved.at[k], up_send.at[k], up_recv.at[k], me ^ k).start()

        @pl.when(k == 0)
        def _():
            copy = pltpu.make_async_copy(stage.at[0], up_moved.at[0], stage_sems.at[0])
            copy.start()
            copy.wait()

        return carry

    lax.fori_loop(0, PEERS, up_step, 0)

    for copy in across:
        copy.wait()
    beside = [remote(windows.at[k], windows.at[k + 1], win_send.at[k + 1], win_recv.at[k + 1], me ^ 1) for k in (0, 2, 4, 6)]
    for copy in beside:
        copy.start()

    def collect(outs):
        def copies(j, buffer):
            for n, (ref, begin, size) in enumerate(outs[j]):
                yield pltpu.make_async_copy(
                    stage.at[buffer, :, pl.ds(begin, size)], ref, stage_sems.at[n * 2 + buffer]
                )

        def step(n, carry):
            buffer = n & 1
            k = n ^ 6

            @pl.when(n >= 2)
            def _():
                for copy in copies(0, buffer):
                    copy.wait()

            gather(k, buffer)
            for j in range(PEERS):

                @pl.when(k == j)
                def _():
                    for copy in copies(j, buffer):
                        copy.start()

            return carry

        lax.fori_loop(0, PEERS, step, 0)
        for buffer in range(2):
            for copy in copies(0, buffer):
                copy.wait()

    loads[1].wait()
    spread_out(rows.at[1], spread)
    collect([[(ref, 0, ref.shape[1])] for ref in gate_rows])

    for copy in beside:
        copy.wait()
    for k in range(PEERS):
        for m in range(2):
            wide[m, k * A_DEV : (k + 1) * A_DEV, :] = windows[k, m * A_DEV : (m + 1) * A_DEV, :]
    depth = COST_ROWS
    group = part.shape[2]

    def cost(j, carry):
        at = pl.ds(pl.multiple_of(j * depth, depth), depth)
        both = [
            lax.dot_general(wide[m], rows[m, at, :], OVER_LANES, preferred_element_type=jnp.float32) for m in range(2)
        ]
        value = both[0] + both[1]
        for k in range(PEERS):
            for c in range(part.shape[0]):
                begin = k * A_DEV + c * group
                part[c, me ^ k, :, at] = value[begin : begin + group]
        return carry

    lax.fori_loop(0, count // depth, cost, 0)
    share = pltpu.make_async_copy(part, partial_ref, part_sem)
    share.start()
    load = pltpu.make_async_copy(down_b, rows.at[0], load_sems.at[0])
    load.start()
    load.wait()
    spread_out(rows.at[0], spread)
    starts = [sum(chunks[:n]) for n in range(len(chunks))]
    collect([[(down_rows[n][k], starts[n], chunks[n]) for n in range(len(chunks))] for k in range(PEERS)])
    share.wait()
    for k in range(1, PEERS):
        remote(up_sent.at[k], up_moved.at[k], up_send.at[k], up_recv.at[k], me ^ k).wait()


def first(up_a, gate_a, up_b, gate_b, down_b, perm, chunks):
    count, features = up_a.shape
    cols = lax.axis_size("cols")
    used = count // LANES
    pad = -(-used // 8) * 8
    slots = count // PEERS
    lanes = -(-slots // LANES) * LANES
    grid = jnp.pad(perm.reshape(used, LANES), ((0, pad - used), (0, 0)), constant_values=PEERS * count)
    vmem = pl.BlockSpec(memory_space=pltpu.VMEM)
    hbm = pl.BlockSpec(memory_space=pltpu.HBM)
    bf16, f32, i32 = jnp.bfloat16, jnp.float32, jnp.int32
    shapes = [
        jax.ShapeDtypeStruct((pad, LANES), i32),
        jax.ShapeDtypeStruct((pad, LANES), i32),
        jax.ShapeDtypeStruct((PEERS, pad, LANES), i32),
        jax.ShapeDtypeStruct((cols, PEERS, A_DEV // cols, count), f32),
        jax.ShapeDtypeStruct((PEERS, slots, features), bf16),
        jax.ShapeDtypeStruct((PEERS, slots, features), bf16),
    ]
    shapes += [jax.ShapeDtypeStruct((slots, size), bf16) for size in (features,) + chunks for _ in range(PEERS)]
    got = pl.pallas_call(
        functools.partial(first_kernel, count, chunks),
        out_shape=shapes,
        in_specs=[vmem] + [hbm] * 5,
        out_specs=[vmem] * 3 + [hbm] * (len(shapes) - 3),
        scratch_shapes=[
            pltpu.VMEM((slots, count), bf16),
            pltpu.VMEM((2 * PEERS, count), bf16),
            pltpu.VMEM((PEERS * pad, LANES), i32),
            pltpu.VMEM((PEERS, 8, lanes), i32),
            pltpu.VMEM((PEERS, 8, lanes), i32),
            pltpu.SMEM((PEERS, 8, lanes), i32),
            pltpu.VMEM((32 * A_DEV, features), bf16),
            pltpu.VMEM((2 * A_DEV, features), bf16),
            pltpu.VMEM((PEERS, 2 * A_DEV, features), bf16),
            pltpu.VMEM((2, A_DEV * PEERS, features), bf16),
            pltpu.VMEM((2, count, features), bf16),
            pltpu.VMEM((count * 8 + 8 * 8, LANES), f32),
            pltpu.VMEM((LANES + 8 * 8, LANES), f32),
            pltpu.VMEM((2, slots, features), bf16),
            pltpu.VMEM((cols, PEERS, A_DEV // cols, count), f32),
        ]
        + [pltpu.SemaphoreType.DMA((PEERS,))] * 6
        + [
            pltpu.SemaphoreType.DMA((2 * A_DEV,)),
            pltpu.SemaphoreType.DMA((2,)),
            pltpu.SemaphoreType.DMA((2 * len(chunks),)),
            pltpu.SemaphoreType.DMA,
            pltpu.SemaphoreType.DMA,
        ],
        compiler_params=pltpu.CompilerParams(
            collective_id=0, has_side_effects=True, vmem_limit_bytes=60 * 1024 * 1024
        ),
    )(grid, up_a, gate_a, up_b, gate_b, down_b)
    code, slot, before, partial_value, up_moved = got[:5]
    lists = [got[6 + n * PEERS : 6 + (n + 1) * PEERS] for n in range(1 + len(chunks))]
    return code, slot, before, partial_value, up_moved, lists


def place_kernel(before_ref, code_ref, initial_ref, *refs):
    *rest, out_ref, held, total = refs
    arrived = rest[-PEERS:]
    t = pl.program_id(0)
    pad = before_ref.shape[0] // PEERS
    last = arrived[0].shape[0] - SLOT
    per = TILE // LANES
    starts, rounds = [], jnp.int32(1)
    for k in range(PEERS):
        lo = before_ref[k * pad + t * per]
        hi = before_ref[k * pad + t * per + per]
        start = lax.shift_left(lax.shift_right_logical(lo, 4), 4)
        starts.append(start)
        rounds = jnp.maximum(rounds, lax.shift_right_logical(hi - start + SLOT - 1, 6))
    lane = lax.broadcasted_iota(jnp.int32, (1, PEERS * SLOT), 1)
    peer = lax.shift_right_logical(lane, 6)
    code = code_ref[...]
    code = code[:, :1]

    def gathered(j):
        first = jnp.zeros_like(lane)
        at = jnp.zeros_like(lane)
        for k in range(PEERS):
            begin = starts[k] + j * SLOT
            from_row = jnp.minimum(begin, last)
            held[k * SLOT : (k + 1) * SLOT, :] = arrived[k][pl.ds(pl.multiple_of(from_row, 16), SLOT), :]
            first = jnp.where(peer == k, begin, first)
            at = jnp.where(peer == k, from_row, at)
        at = at + (lane & (SLOT - 1))
        codes = jnp.where(at >= first, peer * CODE + at, -1)
        return matmul(one_hot(code == codes), held[...])

    total[...] = gathered(jnp.int32(0))

    def more(j, carry):
        total[...] += gathered(j)
        return carry

    lax.fori_loop(1, rounds, more, 0)
    out_ref[...] = ((initial_ref[...].astype(jnp.float32) + total[...]) * 0.5).astype(out_ref.dtype)


def place(before, code, initial, arrived, start, out=None):
    count, features = initial.shape
    slots, size = arrived[0].shape
    wide = lambda t, *_: (t, start // size)
    extra = [] if out is None else [out]
    return pl.pallas_call(
        place_kernel,
        out_shape=jax.ShapeDtypeStruct((count, features), initial.dtype),
        grid_spec=pltpu.PrefetchScalarGridSpec(
            num_scalar_prefetch=1,
            grid=(count // TILE,),
            in_specs=[
                pl.BlockSpec((TILE, LANES), lambda t, *_: (t, 0)),
                pl.BlockSpec((TILE, size), wide),
            ]
            + [pl.BlockSpec(memory_space=pl.ANY)] * len(extra)
            + [pl.BlockSpec((slots, size), lambda t, *_: (0, 0))] * PEERS,
            out_specs=pl.BlockSpec((TILE, size), wide),
            scratch_shapes=[
                pltpu.VMEM((PEERS * SLOT, size), jnp.bfloat16),
                pltpu.VMEM((TILE, size), jnp.float32),
            ],
        ),
        input_output_aliases={3: 0} if extra else {},
        compiler_params=pltpu.CompilerParams(vmem_limit_bytes=60 * 1024 * 1024),
        cost_estimate=pl.CostEstimate(
            flops=2 * count * PEERS * SLOT * size, bytes_accessed=6 * count * size, transcendentals=0
        ),
    )(before, code, initial, *extra, *arrived)


def place_rows_kernel(slot_ref, initial_ref, *refs):
    *arrived, out_ref, spread, turn = refs
    t = pl.program_id(0)
    tall, width = initial_ref.shape
    tiles = width // LANES

    @pl.when(t == 0)
    def _():
        for k in range(PEERS):
            spread_out(arrived[k], spread, k * arrived[k].shape[0] * tiles)

    def step(j, carry):
        at = pl.ds(pl.multiple_of(j * 16, 16), 16)
        for c, tile in sixteen(lambda s: slot_ref[t * tall + j * 16 + s], spread, turn, tiles):
            lanes = slice(c * LANES, (c + 1) * LANES)
            out_ref[at, lanes] = ((initial_ref[at, lanes].astype(jnp.float32) + tile) * 0.5).astype(out_ref.dtype)
        return carry

    lax.fori_loop(0, tall // 16, step, 0)


def place_rows(slot, initial, arrived):
    count, features = initial.shape
    slots = count // PEERS
    if isinstance(arrived, list):
        specs = [pl.BlockSpec((slots, features), lambda t, *_: (0, 0))] * PEERS
    else:
        specs = [pl.BlockSpec((None, slots, features), functools.partial(lambda k, t, *_: (k, 0, 0), k)) for k in range(PEERS)]
        arrived = [arrived] * PEERS
    tall = count // 7 if count % (7 * 16) == 0 else LANES
    return pl.pallas_call(
        place_rows_kernel,
        out_shape=jax.ShapeDtypeStruct((count, features), initial.dtype),
        grid_spec=pltpu.PrefetchScalarGridSpec(
            num_scalar_prefetch=1,
            grid=(count // tall,),
            in_specs=[pl.BlockSpec((tall, features), lambda t, *_: (t, 0))] + specs,
            out_specs=pl.BlockSpec((tall, features), lambda t, *_: (t, 0)),
            scratch_shapes=[
                pltpu.VMEM(((count + 8) * features // LANES, LANES), jnp.float32),
                pltpu.VMEM(((16 + 8) * features // LANES, LANES), jnp.float32),
            ],
        ),
        compiler_params=pltpu.CompilerParams(vmem_limit_bytes=60 * 1024 * 1024),
        cost_estimate=pl.CostEstimate(flops=0, bytes_accessed=6 * count * features, transcendentals=0),
    )(slot, initial, *arrived)


def balanced(up_a, gate_a, down_a, up_b, gate_b, down_b, perm):
    row_count, features = up_a.shape
    cost_scale = (2.0 * D) ** (-0.5)
    chunks = (features // 2, features // 4, features // 4)
    code, slot, before, partial_value, up_moved, lists = first(up_a, gate_a, up_b, gate_b, down_b, perm, chunks)
    before = before[:, :, 0].reshape(-1)
    slot = slot.reshape(-1)
    code = jnp.broadcast_to(code.reshape(-1)[:row_count, None], (row_count, LANES))

    def after(value, *others):
        return lax.optimization_barrier((value,) + others)[0]

    def exchange(rows, ks, *others):
        return {
            k: lax.ppermute(after(rows[k], *others), "rows", [(i, i ^ k) for i in range(PEERS)]) for k in ks
        }

    def parts(rows, *moved):
        got = {0: rows[0]}
        for some in moved:
            got.update(some)
        return [got[k] for k in range(PEERS)]

    gate, down = lists[0], lists[1:]
    gate_first = exchange(gate, (6, 7, 4, 5, 2))
    partial_value = after(partial_value, *(gate[k] for k in (6, 7, 4, 5, 2)))
    shares = lax.all_to_all(partial_value, "cols", split_axis=0, concat_axis=0, tiled=True)
    up_mean = place_rows(slot, up_a, up_moved)
    gate_last = exchange(gate, (3, 1), up_mean)
    left = exchange(down[0], (6, 7, 4, 5, 2, 3, 1), up_mean)
    gate_mean = place_rows(slot, gate_a, parts(gate, gate_first, gate_last))
    middle = exchange(down[1], (6, 7, 4, 5, 2, 3, 1), gate_mean)
    right = exchange(down[2], (6, 7, 4, 5, 2, 3, 1), gate_mean)
    down_mean = place(before, code, down_a, parts(down[0], left), 0)
    down_mean = place(before, code, down_a, parts(down[1], middle), chunks[0], down_mean)
    down_mean = place(before, code, down_a, parts(down[2], right), chunks[0] + chunks[1], down_mean)
    total = (shares[0] + shares[1]) + (shares[2] + shares[3])
    costs = (total.transpose(1, 0, 2).reshape(-1, row_count) * cost_scale).T
    return (costs, up_mean, gate_mean, down_mean)


def pick(array, index):
    rows = jnp.arange(array.shape[0], dtype=jnp.int32)
    hot = (index[:, None] == rows[None, :]).astype(array.dtype)
    return jnp.dot(hot, array, preferred_element_type=jnp.float32).astype(array.dtype)


def mix(initial, picked):
    return ((initial.astype(jnp.float32) + picked.astype(jnp.float32)) * 0.5).astype(jnp.bfloat16)


def general(up_a, gate_a, down_a, up_b, gate_b, down_b, perm):
    row_count, features = up_a.shape
    stride = row_count // A_DEV
    cost_scale = (2.0 * D) ** (-0.5)
    peers = lax.axis_size("rows")
    cols = lax.axis_size("cols")
    capacity = max(2, (row_count + peers - 1) // peers)

    source = perm // row_count
    local_row = perm % row_count
    blocks = jnp.arange(peers, dtype=jnp.int32)
    matches = (source[None, :] == blocks[:, None]).astype(jnp.int32)
    order = jnp.arange(row_count, dtype=jnp.int32)
    ahead = jnp.dot(
        matches.astype(jnp.bfloat16),
        (order[:, None] < order[None, :]).astype(jnp.bfloat16),
        preferred_element_type=jnp.float32,
    )
    arrival_rank = jnp.sum(ahead.astype(jnp.int32) * matches, axis=0)
    high = (local_row // 256).astype(jnp.bfloat16)
    low = (local_row % 256).astype(jnp.bfloat16)
    halves = jnp.stack([high, low])[:, None, :] * matches.astype(jnp.bfloat16)[None]
    at_rank = (arrival_rank[None, :] == jnp.arange(capacity, dtype=jnp.int32)[:, None]).astype(jnp.bfloat16)
    found = jnp.einsum("hsi,ri->hsr", halves, at_rank, preferred_element_type=jnp.float32)
    wanted = found[0].astype(jnp.int32) * 256 + found[1].astype(jnp.int32)
    asked = lax.all_to_all(wanted, "rows", split_axis=0, concat_axis=0, tiled=True).reshape(-1)
    slot = source * capacity + arrival_rank

    window = jnp.concatenate([up_a[::stride], gate_a[::stride]], axis=0)
    pieces = lax.all_gather(window, "rows").reshape(peers, 2, A_DEV, features)
    wide = pieces.transpose(1, 2, 0, 3).reshape(2, A_DEV * peers, features)
    partial_value = jnp.einsum("kd,jd->kj", wide[0], up_b, preferred_element_type=jnp.float32)
    partial_value = partial_value + jnp.einsum("kd,jd->kj", wide[1], gate_b, preferred_element_type=jnp.float32)
    total = lax.psum_scatter(partial_value.reshape(cols, -1, row_count), "cols", scatter_dimension=0)

    def averaged(initial, other):
        moved = pick(other, asked).reshape(peers, capacity, features)
        moved = lax.all_to_all(moved, "rows", split_axis=0, concat_axis=0, tiled=True)
        return mix(initial, pick(moved.reshape(-1, features), slot))

    return (
        (total * cost_scale).T,
        averaged(up_a, up_b),
        averaged(gate_a, gate_b),
        averaged(down_a, down_b),
    )


def solution(mesh):
    def local(up_a, *rest):
        row_count, features = up_a.shape
        even = mesh.shape["rows"] == PEERS and row_count % (PEERS * 16) == 0 and row_count % (A_DEV * 16) == 0
        even = even and row_count % COST_ROWS == 0 and SLOT <= row_count // PEERS < CODE
        even = even and features == 8 * LANES and mesh.shape["cols"] == A_DEV // 8
        return (balanced if even else general)(up_a, *rest)

    placed = (P("rows", "cols"),) * 6 + (P("rows"),)
    return jax.shard_map(
        local,
        mesh=mesh,
        in_specs=placed,
        out_specs=(P("rows", "cols"),) * 4,
        check_vma=False,
    )
```

```python
import functools

import jax
import jax.numpy as jnp
from jax import lax
from jax.experimental import pallas as pl
from jax.experimental.pallas import tpu as pltpu
from jax.sharding import PartitionSpec as P

D = 4096
A_DEV = 32
MESH = pl.DeviceIdType.MESH

PEERS = 8
LANES = 128
TILE = 256
SLOT = 64
ORDER = (6, 7, 4, 5, 2, 3, 1)
AHEAD = 5
TALL = 512
ROWS = 32
COST_ROWS = 512
OVER_LANES = (((1,), (1,)), ((), ()))
CODE = 1024


def one_hot(hit):
    return jnp.where(hit, 1.0, 0.0).astype(jnp.bfloat16)


def matmul(a, b):
    return jnp.dot(a, b, preferred_element_type=jnp.float32)


def count_ranks(count, me, perm_ref, code_ref, slot_ref, before_ref, hot, halves, counts, sent):
    pad = perm_ref.shape[0]
    used = count // LANES
    slots = count // PEERS
    perm = perm_ref[...]
    source = jnp.zeros_like(perm)
    for k in range(1, PEERS + 1):
        source = source + jnp.where(perm >= k * count, 1, 0)
    row = perm - source * count
    masks = jnp.concatenate([jnp.where(source == k, 1.0, 0.0) for k in range(PEERS)], axis=0)
    packed = masks.astype(jnp.bfloat16)
    shape = (LANES, LANES)
    lane_before = one_hot(lax.broadcasted_iota(jnp.int32, shape, 0) < lax.broadcasted_iota(jnp.int32, shape, 1))
    within = matmul(packed, lane_before)
    totals = matmul(packed, jnp.ones(shape, jnp.bfloat16)).astype(jnp.bfloat16)
    shape = (PEERS * pad, PEERS * pad)
    left, right = lax.broadcasted_iota(jnp.int32, shape, 0), lax.broadcasted_iota(jnp.int32, shape, 1)
    row_before = one_hot((right < left) & (right >= left - lax.rem(left, pad)))
    ahead = matmul(row_before, totals)
    counts[...] = ahead.astype(jnp.int32)
    ranked = masks * (within + ahead)
    rank = ranked[:pad]
    for k in range(1, PEERS):
        rank = rank + ranked[k * pad : (k + 1) * pad]
    rank = rank.astype(jnp.int32)
    code_ref[...] = (source ^ me) * CODE + rank
    slot_ref[...] = first_of(jnp.minimum((source ^ me) * slots + rank, count - 1), 8)
    for k in range(PEERS):
        before_ref[k] = counts[pl.ds(pl.multiple_of((me ^ k) * pad, pad), pad), :]

    high = lax.shift_right_logical(row, 8).astype(jnp.float32)
    low = (row & 255).astype(jnp.float32)
    block = lax.broadcasted_iota(jnp.int32, (PEERS, LANES), 0)
    slot = lax.broadcasted_iota(jnp.int32, (slots, LANES), 0)
    for j in range(used):
        at = slice(j * LANES, (j + 1) * LANES)
        one = slice(j, j + 1)
        mine = source[one] == block
        both = [jnp.where(mine, part[one], 0.0) for part in (high, low)]
        halves[:, at] = jnp.concatenate(both, axis=0).astype(jnp.bfloat16)
        hot[:, at] = one_hot(rank[one] == slot)
    found = lax.dot_general(halves[...], hot[...], OVER_LANES, preferred_element_type=jnp.float32)
    wanted = found[:PEERS] * 256.0 + found[PEERS:]
    for k in range(PEERS):
        sent[k, :, :slots] = jnp.broadcast_to(wanted[k : k + 1], (8, slots)).astype(jnp.int32)
        sent[k, :, slots:] = jnp.zeros((8, sent.shape[2] - slots), jnp.int32)


def spread_out(rows_ref, spread, base=0):
    tall, width = rows_ref.shape
    tiles = width // LANES

    def step(m, carry):
        for c in range(tiles):
            v = rows_ref[pl.ds(pl.multiple_of(m * 16, 16), 16), c * LANES : (c + 1) * LANES].astype(jnp.float32)
            for h in range(2):
                to = base + (m * 2 + h) * 8 * tiles + c * 8
                spread[pl.ds(pl.multiple_of(to, 8), 8), :] = v[h * 8 : h * 8 + 8]
        return carry

    lax.fori_loop(0, tall // 16, step, 0)


def first_of(row, tiles):
    return lax.shift_right_logical(row, 3) * (8 * tiles) + (row & 7)


def rows_of(begin_of, spread, turn, tiles):
    for s in range(ROWS):
        to = (s // 8) * 8 * tiles + s % 8
        turn[pl.ds(to, tiles, stride=8), :] = spread[pl.ds(begin_of(s), tiles, stride=8), :]
    for h in range(ROWS // 16):
        for c in range(tiles):
            both = [turn[pl.ds(((2 * h + half) * tiles + c) * 8, 8), :] for half in range(2)]
            yield h * 16, c, jnp.concatenate(both, axis=0)


def first_kernel(count, chunks, perm_ref, up_a, gate_a, up_b, gate_b, down_b, code_ref, slot_ref, before_ref, partial_ref, up_moved, up_sent, *refs):
    gate_rows, refs = refs[:PEERS], refs[PEERS:]
    down_rows = [refs[n * PEERS : (n + 1) * PEERS] for n in range(len(chunks))]
    refs = refs[len(chunks) * PEERS :]
    hot, halves, counts, sent, got, asked, held, window, windows, wide, rows, spread, turn, stage, part = refs[:15]
    ask_send, ask_recv, up_send, up_recv, win_send, win_recv, strip_sems, load_sems, stage_sems, own_sem, part_sem = refs[15:]
    me = lax.axis_index("rows")
    slots = count // PEERS
    stride = count // A_DEV
    barrier = pltpu.get_barrier_semaphore()
    for k in range(1, PEERS):
        pl.semaphore_signal(barrier, inc=1, device_id={"rows": me ^ k}, device_id_type=MESH)

    strips = []
    for m, ref in enumerate((up_a, gate_a)):
        for i in range(A_DEV):
            at = m * A_DEV + i
            strips.append(
                pltpu.make_async_copy(ref.at[pl.ds(i * stride, 16)], held.at[pl.ds(at * 16, 16)], strip_sems.at[at])
            )
    for copy in strips:
        copy.start()
    loads = [pltpu.make_async_copy(ref, rows.at[n], load_sems.at[n]) for n, ref in enumerate((up_b, gate_b))]
    for copy in loads:
        copy.start()

    for copy in strips:
        copy.wait()
    shape = (2 * A_DEV, 32 * A_DEV)
    first = lax.broadcasted_iota(jnp.int32, shape, 0) * 16 == lax.broadcasted_iota(jnp.int32, shape, 1)
    window[...] = matmul(one_hot(first), held[...]).astype(jnp.bfloat16)
    windows[0] = window[...]
    pl.semaphore_wait(barrier, PEERS - 1)

    def remote(src, dst, send, recv, peer):
        return pltpu.make_async_remote_copy(
            src_ref=src, dst_ref=dst, send_sem=send, recv_sem=recv, device_id={"rows": peer}, device_id_type=MESH
        )

    across = [
        remote(window, windows.at[k], win_send.at[k], win_recv.at[k], me ^ k) for k in (6, 2, 4)
    ]
    for copy in across:
        copy.start()

    count_ranks(count, me, perm_ref, code_ref, slot_ref, before_ref, hot, halves, counts, sent)
    asks = [remote(sent.at[me ^ k], got.at[k], ask_send.at[k], ask_recv.at[k], me ^ k) for k in (6, 7, 4, 5, 2, 3, 1)]
    for copy in asks:
        copy.start()
    own = pltpu.make_async_copy(sent.at[me], got.at[0], own_sem)
    own.start()
    loads[0].wait()
    spread_out(rows.at[0], spread)
    own.wait()
    for copy in asks:
        copy.wait()
    got[...] = first_of(jnp.clip(got[...], 0, count - 1), 8)
    own = pltpu.make_async_copy(got, asked, own_sem)
    own.start()
    own.wait()

    def gather(k, buffer):
        def step(t, carry):
            for row, c, tile in rows_of(lambda s: asked[k, 0, t * ROWS + s], spread, turn, 8):
                at = pl.ds(pl.multiple_of(t * ROWS + row, 16), 16)
                stage[buffer, at, c * LANES : (c + 1) * LANES] = tile.astype(jnp.bfloat16)
            return carry

        lax.fori_loop(0, slots // ROWS, step, 0)

    def up_step(n, carry):
        k = n ^ 6
        gather(k, 0)

        @pl.when(k > 0)
        def _():
            copy = pltpu.make_async_copy(stage.at[0], up_sent.at[k], stage_sems.at[0])
            copy.start()
            copy.wait()
            remote(up_sent.at[k], up_moved.at[k], up_send.at[k], up_recv.at[k], me ^ k).start()

        @pl.when(k == 0)
        def _():
            copy = pltpu.make_async_copy(stage.at[0], up_moved.at[0], stage_sems.at[0])
            copy.start()
            copy.wait()

        return carry

    lax.fori_loop(0, PEERS, up_step, 0)

    for copy in across:
        copy.wait()
    beside = [remote(windows.at[k], windows.at[k + 1], win_send.at[k + 1], win_recv.at[k + 1], me ^ 1) for k in (0, 2, 4, 6)]
    for copy in beside:
        copy.start()

    def collect(outs):
        def copies(j, buffer):
            for n, (ref, begin, size) in enumerate(outs[j]):
                yield pltpu.make_async_copy(
                    stage.at[buffer, :, pl.ds(begin, size)], ref, stage_sems.at[n * 2 + buffer]
                )

        def step(n, carry):
            buffer = n & 1
            k = n ^ 6

            @pl.when(n >= 2)
            def _():
                for copy in copies(0, buffer):
                    copy.wait()

            gather(k, buffer)
            for j in range(PEERS):

                @pl.when(k == j)
                def _():
                    for copy in copies(j, buffer):
                        copy.start()

            return carry

        lax.fori_loop(0, PEERS, step, 0)
        for buffer in range(2):
            for copy in copies(0, buffer):
                copy.wait()

    loads[1].wait()
    spread_out(rows.at[1], spread)
    collect([[(ref, 0, ref.shape[1])] for ref in gate_rows])

    for copy in beside:
        copy.wait()
    for k in range(PEERS):
        for m in range(2):
            wide[m, k * A_DEV : (k + 1) * A_DEV, :] = windows[k, m * A_DEV : (m + 1) * A_DEV, :]
    depth = COST_ROWS
    group = part.shape[2]

    def cost(j, carry):
        at = pl.ds(pl.multiple_of(j * depth, depth), depth)
        both = [
            lax.dot_general(wide[m], rows[m, at, :], OVER_LANES, preferred_element_type=jnp.float32) for m in range(2)
        ]
        value = both[0] + both[1]
        for k in range(PEERS):
            for c in range(part.shape[0]):
                begin = k * A_DEV + c * group
                part[c, me ^ k, :, at] = value[begin : begin + group]
        return carry

    lax.fori_loop(0, count // depth, cost, 0)
    share = pltpu.make_async_copy(part, partial_ref, part_sem)
    share.start()
    load = pltpu.make_async_copy(down_b, rows.at[0], load_sems.at[0])
    load.start()
    load.wait()
    spread_out(rows.at[0], spread)
    starts = [sum(chunks[:n]) for n in range(len(chunks))]
    collect([[(down_rows[n][k], starts[n], chunks[n]) for n in range(len(chunks))] for k in range(PEERS)])
    share.wait()
    for k in range(1, PEERS):
        remote(up_sent.at[k], up_moved.at[k], up_send.at[k], up_recv.at[k], me ^ k).wait()


def first(up_a, gate_a, up_b, gate_b, down_b, perm, chunks):
    count, features = up_a.shape
    cols = lax.axis_size("cols")
    used = count // LANES
    pad = -(-used // 8) * 8
    slots = count // PEERS
    lanes = -(-slots // LANES) * LANES
    grid = jnp.pad(perm.reshape(used, LANES), ((0, pad - used), (0, 0)), constant_values=PEERS * count)
    vmem = pl.BlockSpec(memory_space=pltpu.VMEM)
    hbm = pl.BlockSpec(memory_space=pltpu.HBM)
    bf16, f32, i32 = jnp.bfloat16, jnp.float32, jnp.int32
    shapes = [
        jax.ShapeDtypeStruct((pad, LANES), i32),
        jax.ShapeDtypeStruct((pad, LANES), i32),
        jax.ShapeDtypeStruct((PEERS, pad, LANES), i32),
        jax.ShapeDtypeStruct((cols, PEERS, A_DEV // cols, count), f32),
        jax.ShapeDtypeStruct((PEERS, slots, features), bf16),
        jax.ShapeDtypeStruct((PEERS, slots, features), bf16),
    ]
    shapes += [jax.ShapeDtypeStruct((slots, size), bf16) for size in (features,) + chunks for _ in range(PEERS)]
    got = pl.pallas_call(
        functools.partial(first_kernel, count, chunks),
        out_shape=shapes,
        in_specs=[vmem] + [hbm] * 5,
        out_specs=[vmem] * 3 + [hbm] * (len(shapes) - 3),
        scratch_shapes=[
            pltpu.VMEM((slots, count), bf16),
            pltpu.VMEM((2 * PEERS, count), bf16),
            pltpu.VMEM((PEERS * pad, LANES), i32),
            pltpu.VMEM((PEERS, 8, lanes), i32),
            pltpu.VMEM((PEERS, 8, lanes), i32),
            pltpu.SMEM((PEERS, 8, lanes), i32),
            pltpu.VMEM((32 * A_DEV, features), bf16),
            pltpu.VMEM((2 * A_DEV, features), bf16),
            pltpu.VMEM((PEERS, 2 * A_DEV, features), bf16),
            pltpu.VMEM((2, A_DEV * PEERS, features), bf16),
            pltpu.VMEM((2, count, features), bf16),
            pltpu.VMEM((count * 8 + 8 * 8, LANES), f32),
            pltpu.VMEM(((ROWS + 8) * 8, LANES), f32),
            pltpu.VMEM((2, slots, features), bf16),
            pltpu.VMEM((cols, PEERS, A_DEV // cols, count), f32),
        ]
        + [pltpu.SemaphoreType.DMA((PEERS,))] * 6
        + [
            pltpu.SemaphoreType.DMA((2 * A_DEV,)),
            pltpu.SemaphoreType.DMA((2,)),
            pltpu.SemaphoreType.DMA((2 * len(chunks),)),
            pltpu.SemaphoreType.DMA,
            pltpu.SemaphoreType.DMA,
        ],
        compiler_params=pltpu.CompilerParams(
            collective_id=0, has_side_effects=True, vmem_limit_bytes=60 * 1024 * 1024
        ),
    )(grid, up_a, gate_a, up_b, gate_b, down_b)
    code, slot, before, partial_value, up_moved = got[:5]
    lists = [got[6 + n * PEERS : 6 + (n + 1) * PEERS] for n in range(1 + len(chunks))]
    return code, slot, before, partial_value, up_moved, lists


def place_kernel(before_ref, code_ref, initial_ref, *refs):
    *rest, out_ref, held, total = refs
    arrived = rest[-PEERS:]
    t = pl.program_id(0)
    pad = before_ref.shape[0] // PEERS
    last = arrived[0].shape[0] - SLOT
    per = TILE // LANES
    starts, rounds = [], jnp.int32(1)
    for k in range(PEERS):
        lo = before_ref[k * pad + t * per]
        hi = before_ref[k * pad + t * per + per]
        start = lax.shift_left(lax.shift_right_logical(lo, 4), 4)
        starts.append(start)
        rounds = jnp.maximum(rounds, lax.shift_right_logical(hi - start + SLOT - 1, 6))
    lane = lax.broadcasted_iota(jnp.int32, (1, PEERS * SLOT), 1)
    peer = lax.shift_right_logical(lane, 6)
    code = code_ref[...]
    code = code[:, :1]

    def gathered(j):
        first = jnp.zeros_like(lane)
        at = jnp.zeros_like(lane)
        for k in range(PEERS):
            begin = starts[k] + j * SLOT
            from_row = jnp.minimum(begin, last)
            held[k * SLOT : (k + 1) * SLOT, :] = arrived[k][pl.ds(pl.multiple_of(from_row, 16), SLOT), :]
            first = jnp.where(peer == k, begin, first)
            at = jnp.where(peer == k, from_row, at)
        at = at + (lane & (SLOT - 1))
        codes = jnp.where(at >= first, peer * CODE + at, -1)
        return matmul(one_hot(code == codes), held[...])

    total[...] = gathered(jnp.int32(0))

    def more(j, carry):
        total[...] += gathered(j)
        return carry

    lax.fori_loop(1, rounds, more, 0)
    out_ref[...] = ((initial_ref[...].astype(jnp.float32) + total[...]) * 0.5).astype(out_ref.dtype)


def place(before, code, initial, arrived, start, out=None):
    count, features = initial.shape
    slots, size = arrived[0].shape
    wide = lambda t, *_: (t, start // size)
    extra = [] if out is None else [out]
    return pl.pallas_call(
        place_kernel,
        out_shape=jax.ShapeDtypeStruct((count, features), initial.dtype),
        grid_spec=pltpu.PrefetchScalarGridSpec(
            num_scalar_prefetch=1,
            grid=(count // TILE,),
            in_specs=[
                pl.BlockSpec((TILE, LANES), lambda t, *_: (t, 0)),
                pl.BlockSpec((TILE, size), wide),
            ]
            + [pl.BlockSpec(memory_space=pl.ANY)] * len(extra)
            + [pl.BlockSpec((slots, size), lambda t, *_: (0, 0))] * PEERS,
            out_specs=pl.BlockSpec((TILE, size), wide),
            scratch_shapes=[
                pltpu.VMEM((PEERS * SLOT, size), jnp.bfloat16),
                pltpu.VMEM((TILE, size), jnp.float32),
            ],
        ),
        input_output_aliases={3: 0} if extra else {},
        compiler_params=pltpu.CompilerParams(vmem_limit_bytes=60 * 1024 * 1024),
        cost_estimate=pl.CostEstimate(
            flops=2 * count * PEERS * SLOT * size, bytes_accessed=6 * count * size, transcendentals=0
        ),
    )(before, code, initial, *extra, *arrived)


def place_rows_kernel(slot_ref, initial_ref, *refs):
    *arrived, out_ref, spread, turn = refs
    t = pl.program_id(0)
    tall, width = initial_ref.shape
    tiles = width // LANES

    @pl.when(t == 0)
    def _():
        for k in range(PEERS):
            spread_out(arrived[k], spread, k * arrived[k].shape[0] * tiles)

    def step(j, carry):
        for row, c, tile in rows_of(lambda s: slot_ref[t * tall + j * ROWS + s], spread, turn, tiles):
            at = pl.ds(pl.multiple_of(j * ROWS + row, 16), 16)
            lanes = slice(c * LANES, (c + 1) * LANES)
            out_ref[at, lanes] = ((initial_ref[at, lanes].astype(jnp.float32) + tile) * 0.5).astype(out_ref.dtype)
        return carry

    lax.fori_loop(0, tall // ROWS, step, 0)


def place_rows(slot, initial, arrived):
    count, features = initial.shape
    slots = count // PEERS
    if isinstance(arrived, list):
        specs = [pl.BlockSpec((slots, features), lambda t, *_: (0, 0))] * PEERS
    else:
        specs = [pl.BlockSpec((None, slots, features), functools.partial(lambda k, t, *_: (k, 0, 0), k)) for k in range(PEERS)]
        arrived = [arrived] * PEERS
    tall = TALL
    return pl.pallas_call(
        place_rows_kernel,
        out_shape=jax.ShapeDtypeStruct((count, features), initial.dtype),
        grid_spec=pltpu.PrefetchScalarGridSpec(
            num_scalar_prefetch=1,
            grid=(count // tall,),
            in_specs=[pl.BlockSpec((tall, features), lambda t, *_: (t, 0))] + specs,
            out_specs=pl.BlockSpec((tall, features), lambda t, *_: (t, 0)),
            scratch_shapes=[
                pltpu.VMEM(((count + 8) * features // LANES, LANES), jnp.float32),
                pltpu.VMEM(((ROWS + 8) * features // LANES, LANES), jnp.float32),
            ],
        ),
        compiler_params=pltpu.CompilerParams(vmem_limit_bytes=60 * 1024 * 1024),
        cost_estimate=pl.CostEstimate(flops=0, bytes_accessed=6 * count * features, transcendentals=0),
    )(slot, initial, *arrived)


def balanced(up_a, gate_a, down_a, up_b, gate_b, down_b, perm):
    row_count, features = up_a.shape
    cost_scale = (2.0 * D) ** (-0.5)
    chunks = (features // 2, features // 4, features // 4)
    code, slot, before, partial_value, up_moved, lists = first(up_a, gate_a, up_b, gate_b, down_b, perm, chunks)
    before = before[:, :, 0].reshape(-1)
    slot = slot.reshape(-1)
    code = jnp.broadcast_to(code.reshape(-1)[:row_count, None], (row_count, LANES))

    def after(value, *others):
        return lax.optimization_barrier((value,) + others)[0]

    gate, down = lists[0], lists[1:]
    arrived = []

    def travel(rows, ks, *others):
        for k in ks:
            before_it = arrived[-AHEAD:][:1] if len(arrived) >= AHEAD else []
            sent = after(rows[k], *before_it, *others)
            arrived.append(lax.ppermute(sent, "rows", [(i, i ^ k) for i in range(PEERS)]))

    def taken(rows, at):
        got = {0: rows[0], **dict(zip(ORDER, arrived[at : at + len(ORDER)]))}
        return [got[k] for k in range(PEERS)]

    travel(gate, ORDER)
    shares = lax.all_to_all(after(partial_value, arrived[2]), "cols", split_axis=0, concat_axis=0, tiled=True)
    up_mean = place_rows(after(slot, arrived[2]), up_a, up_moved)
    travel(down[0], ORDER[:1], up_mean)
    travel(down[0], ORDER[1:AHEAD])
    gate_mean = place_rows(slot, gate_a, taken(gate, 0))
    travel(down[0], ORDER[AHEAD : AHEAD + 1], gate_mean)
    travel(down[0], ORDER[AHEAD + 1 :])
    travel(down[1], ORDER[:AHEAD])
    down_mean = place(before, code, down_a, taken(down[0], 7), 0)
    total = (shares[0] + shares[1]) + (shares[2] + shares[3])
    costs = (total.transpose(1, 0, 2).reshape(-1, row_count) * cost_scale).T
    travel(down[1], ORDER[AHEAD : AHEAD + 1], down_mean)
    travel(down[1], ORDER[AHEAD + 1 :])
    travel(down[2], ORDER[:AHEAD])
    down_mean = place(before, code, down_a, taken(down[1], 14), chunks[0], down_mean)
    travel(down[2], ORDER[AHEAD : AHEAD + 1], down_mean, costs)
    travel(down[2], ORDER[AHEAD + 1 :])
    down_mean = place(before, code, down_a, taken(down[2], 21), chunks[0] + chunks[1], down_mean)
    return (costs, up_mean, gate_mean, down_mean)


def pick(array, index):
    rows = jnp.arange(array.shape[0], dtype=jnp.int32)
    hot = (index[:, None] == rows[None, :]).astype(array.dtype)
    return jnp.dot(hot, array, preferred_element_type=jnp.float32).astype(array.dtype)


def mix(initial, picked):
    return ((initial.astype(jnp.float32) + picked.astype(jnp.float32)) * 0.5).astype(jnp.bfloat16)


def general(up_a, gate_a, down_a, up_b, gate_b, down_b, perm):
    row_count, features = up_a.shape
    stride = row_count // A_DEV
    cost_scale = (2.0 * D) ** (-0.5)
    peers = lax.axis_size("rows")
    cols = lax.axis_size("cols")
    capacity = max(2, (row_count + peers - 1) // peers)

    source = perm // row_count
    local_row = perm % row_count
    blocks = jnp.arange(peers, dtype=jnp.int32)
    matches = (source[None, :] == blocks[:, None]).astype(jnp.int32)
    order = jnp.arange(row_count, dtype=jnp.int32)
    ahead = jnp.dot(
        matches.astype(jnp.bfloat16),
        (order[:, None] < order[None, :]).astype(jnp.bfloat16),
        preferred_element_type=jnp.float32,
    )
    arrival_rank = jnp.sum(ahead.astype(jnp.int32) * matches, axis=0)
    high = (local_row // 256).astype(jnp.bfloat16)
    low = (local_row % 256).astype(jnp.bfloat16)
    halves = jnp.stack([high, low])[:, None, :] * matches.astype(jnp.bfloat16)[None]
    at_rank = (arrival_rank[None, :] == jnp.arange(capacity, dtype=jnp.int32)[:, None]).astype(jnp.bfloat16)
    found = jnp.einsum("hsi,ri->hsr", halves, at_rank, preferred_element_type=jnp.float32)
    wanted = found[0].astype(jnp.int32) * 256 + found[1].astype(jnp.int32)
    asked = lax.all_to_all(wanted, "rows", split_axis=0, concat_axis=0, tiled=True).reshape(-1)
    slot = source * capacity + arrival_rank

    window = jnp.concatenate([up_a[::stride], gate_a[::stride]], axis=0)
    pieces = lax.all_gather(window, "rows").reshape(peers, 2, A_DEV, features)
    wide = pieces.transpose(1, 2, 0, 3).reshape(2, A_DEV * peers, features)
    partial_value = jnp.einsum("kd,jd->kj", wide[0], up_b, preferred_element_type=jnp.float32)
    partial_value = partial_value + jnp.einsum("kd,jd->kj", wide[1], gate_b, preferred_element_type=jnp.float32)
    total = lax.psum_scatter(partial_value.reshape(cols, -1, row_count), "cols", scatter_dimension=0)

    def averaged(initial, other):
        moved = pick(other, asked).reshape(peers, capacity, features)
        moved = lax.all_to_all(moved, "rows", split_axis=0, concat_axis=0, tiled=True)
        return mix(initial, pick(moved.reshape(-1, features), slot))

    return (
        (total * cost_scale).T,
        averaged(up_a, up_b),
        averaged(gate_a, gate_b),
        averaged(down_a, down_b),
    )


def solution(mesh):
    def local(up_a, *rest):
        row_count, features = up_a.shape
        even = mesh.shape["rows"] == PEERS and row_count % (PEERS * 16) == 0 and row_count % (A_DEV * 16) == 0
        even = even and row_count % COST_ROWS == 0 and row_count % TALL == 0 and row_count % (PEERS * ROWS) == 0
        even = even and SLOT <= row_count // PEERS < CODE
        even = even and features == 8 * LANES and mesh.shape["cols"] == A_DEV // 8
        return (balanced if even else general)(up_a, *rest)

    placed = (P("rows", "cols"),) * 6 + (P("rows"),)
    return jax.shard_map(
        local,
        mesh=mesh,
        in_specs=placed,
        out_specs=(P("rows", "cols"),) * 4,
        check_vma=False,
    )
```

```python
import functools

import jax
import jax.numpy as jnp
from jax import lax
from jax.experimental import pallas as pl
from jax.experimental.pallas import tpu as pltpu
from jax.sharding import PartitionSpec as P

D = 4096
A_DEV = 32
MESH = pl.DeviceIdType.MESH

PEERS = 8
LANES = 128
ORDER = (6, 7, 4, 5, 2, 3, 1)
LATER = (2, 4, 3, 5, 1, 6, 7)
AHEAD = 9
ROWS = 32
COST_ROWS = 512
PARTS = 4
OVER_LANES = (((1,), (1,)), ((), ()))


def one_hot(hit):
    return jnp.where(hit, 1.0, 0.0).astype(jnp.bfloat16)


def matmul(a, b):
    return jnp.dot(a, b, preferred_element_type=jnp.float32)


def count_ranks(count, me, perm_ref, slot_ref, hot, halves, padded, sent):
    used, pad = perm_ref.shape[0], padded.shape[0]
    slots = count // PEERS
    padded[...] = jnp.full(padded.shape, PEERS * count, jnp.int32)
    padded[:used] = perm_ref[...]
    perm = padded[...]
    source = jnp.zeros_like(perm)
    for k in range(1, PEERS + 1):
        source = source + jnp.where(perm >= k * count, 1, 0)
    row = perm - source * count
    masks = jnp.concatenate([jnp.where(source == k, 1.0, 0.0) for k in range(PEERS)], axis=0)
    packed = masks.astype(jnp.bfloat16)
    shape = (LANES, LANES)
    lane_before = one_hot(lax.broadcasted_iota(jnp.int32, shape, 0) < lax.broadcasted_iota(jnp.int32, shape, 1))
    within = matmul(packed, lane_before)
    totals = matmul(packed, jnp.ones(shape, jnp.bfloat16)).astype(jnp.bfloat16)
    shape = (PEERS * pad, PEERS * pad)
    left, right = lax.broadcasted_iota(jnp.int32, shape, 0), lax.broadcasted_iota(jnp.int32, shape, 1)
    row_before = one_hot((right < left) & (right >= left - lax.rem(left, pad)))
    ahead = matmul(row_before, totals)
    ranked = masks * (within + ahead)
    rank = ranked[:pad]
    for k in range(1, PEERS):
        rank = rank + ranked[k * pad : (k + 1) * pad]
    rank = rank.astype(jnp.int32)
    slot_ref[...] = jnp.clip((source ^ me) * slots + rank, 0, count - 1)

    high = lax.shift_right_logical(row, 8).astype(jnp.float32)
    low = (row & 255).astype(jnp.float32)
    block = lax.broadcasted_iota(jnp.int32, (PEERS, LANES), 0)
    slot = lax.broadcasted_iota(jnp.int32, (slots, LANES), 0)
    for j in range(used):
        at = slice(j * LANES, (j + 1) * LANES)
        one = slice(j, j + 1)
        mine = source[one] == block
        both = [jnp.where(mine, part[one], 0.0) for part in (high, low)]
        halves[:, at] = jnp.concatenate(both, axis=0).astype(jnp.bfloat16)
        hot[:, at] = one_hot(rank[one] == slot)
    found = lax.dot_general(halves[...], hot[...], OVER_LANES, preferred_element_type=jnp.float32)
    wanted = found[:PEERS] * 256.0 + found[PEERS:]
    for k in range(PEERS):
        sent[k, :, :slots] = jnp.broadcast_to(wanted[k : k + 1], (8, slots)).astype(jnp.int32)
        sent[k, :, slots:] = jnp.zeros((8, sent.shape[2] - slots), jnp.int32)


def spread_out(rows_ref, spread, tiles=None):
    tall, width = rows_ref.shape
    tiles = tiles or width // LANES

    def step(m, carry):
        for c in range(tiles):
            v = rows_ref[pl.ds(pl.multiple_of(m * 16, 16), 16), c * LANES : (c + 1) * LANES].astype(jnp.float32)
            for h in range(2):
                to = (m * 2 + h) * 8 * tiles + c * 8
                spread[pl.ds(pl.multiple_of(to, 8), 8), :] = v[h * 8 : h * 8 + 8]
        return carry

    lax.fori_loop(0, tall // 16, step, 0)


def first_of(row, tiles):
    return lax.shift_right_logical(row, 3) * (8 * tiles) + (row & 7)


def rows_of(begin_of, spread, turn, tiles):
    for s in range(ROWS):
        to = (s // 8) * 8 * tiles + s % 8
        turn[pl.ds(to, tiles, stride=8), :] = spread[pl.ds(begin_of(s), tiles, stride=8), :]
    for h in range(ROWS // 16):
        for c in range(tiles):
            both = [turn[pl.ds(((2 * h + half) * tiles + c) * 8, 8), :] for half in range(2)]
            yield h * 16, c, jnp.concatenate(both, axis=0)


def table_reader(table):
    per = LANES // ROWS

    def read(j, s):
        return table[lax.div(j, per), lax.rem(j, per) * ROWS + s]

    return read


def main_kernel(count, cut, perm_ref, up_a, gate_a, down_a, up_b, gate_b, down_b, *refs):
    begin_ref, means, costs_ref, refs = refs[0], refs[1:4], refs[4], refs[5:]
    sent, moved, refs = refs[:4], refs[4:8], refs[8:]
    hot, halves, padded, slot, table, begins, ask, got, asked, held, window, windows, wide, rows, spread, turn, stage = refs[:17]
    part, shares, refs = refs[17], refs[18], refs[19:]
    ask_send, ask_recv, win_send, win_recv, item_send, item_recv, share_send, share_recv, strip_sems, load_sems, stage_sems, own_sem = refs
    me, column = lax.axis_index("rows"), lax.axis_index("cols")
    slots = count // PEERS
    stride = count // A_DEV
    cols = part.shape[0]
    features = up_a.shape[1]
    widths = (features, features, cut, features - cut)
    barrier = pltpu.get_barrier_semaphore()
    for k in range(1, PEERS):
        pl.semaphore_signal(barrier, inc=1, device_id={"rows": me ^ k}, device_id_type=MESH)
    for k in range(1, cols):
        pl.semaphore_signal(barrier, inc=1, device_id={"cols": column ^ k}, device_id_type=MESH)

    strips = []
    for m, ref in enumerate((up_a, gate_a)):
        for i in range(A_DEV):
            at = m * A_DEV + i
            strips.append(
                pltpu.make_async_copy(ref.at[pl.ds(i * stride, 16)], held.at[pl.ds(at * 16, 16)], strip_sems.at[at])
            )
    for copy in strips:
        copy.start()
    loads = [pltpu.make_async_copy(ref, rows.at[n], load_sems.at[n]) for n, ref in enumerate((up_b, gate_b))]
    for copy in loads:
        copy.start()

    for copy in strips:
        copy.wait()
    shape = (2 * A_DEV, 32 * A_DEV)
    first = lax.broadcasted_iota(jnp.int32, shape, 0) * 16 == lax.broadcasted_iota(jnp.int32, shape, 1)
    window[...] = matmul(one_hot(first), held[...]).astype(jnp.bfloat16)
    windows[0] = window[...]
    pl.semaphore_wait(barrier, PEERS - 1 + cols - 1)

    def remote(src, dst, send, recv, peer, axis="rows"):
        return pltpu.make_async_remote_copy(
            src_ref=src, dst_ref=dst, send_sem=send, recv_sem=recv, device_id={axis: peer}, device_id_type=MESH
        )

    across = [remote(window, windows.at[k], win_send.at[k], win_recv.at[k], me ^ k) for k in (6, 2, 4)]
    for copy in across:
        copy.start()

    count_ranks(count, me, perm_ref, slot, hot, halves, padded, ask)
    asks = [remote(ask.at[me ^ k], got.at[k], ask_send.at[k], ask_recv.at[k], me ^ k) for k in ORDER]
    for copy in asks:
        copy.start()
    own = pltpu.make_async_copy(ask.at[me], got.at[0], own_sem)
    own.start()
    begin_ref[...] = first_of(slot[...], widths[3] // LANES)
    loads[0].wait()
    spread_out(rows.at[0], spread)
    own.wait()
    for copy in asks:
        copy.wait()
    got[...] = first_of(jnp.clip(got[...], 0, count - 1), features // LANES)
    own = pltpu.make_async_copy(got, asked, own_sem)
    own.start()
    own.wait()

    def gather(k, buffer):
        def step(t, carry):
            for row, c, tile in rows_of(lambda s: asked[k, 0, t * ROWS + s], spread, turn, features // LANES):
                at = pl.ds(pl.multiple_of(t * ROWS + row, 16), 16)
                stage[buffer, at, c * LANES : (c + 1) * LANES] = tile.astype(jnp.bfloat16)
            return carry

        lax.fori_loop(0, slots // ROWS, step, 0)

    items = [(a, k) for a in range(4) for k in (ORDER if a < 2 else LATER)]

    def item(a, k):
        return remote(sent[a].at[k], moved[a].at[k], item_send.at[a, k], item_recv.at[a, k], me ^ k)

    def up_step(n, carry):
        k = n ^ 6
        gather(k, 0)
        copy = pltpu.make_async_copy(stage.at[0], sent[0].at[k], stage_sems.at[0])
        copy.start()
        copy.wait()

        @pl.when(k > 0)
        def _():
            item(0, k).start()

        return carry

    lax.fori_loop(0, PEERS, up_step, 0)
    done = {"sent": len(ORDER), "here": 0}

    def push(count_of):
        while done["sent"] < count_of:
            item(*items[done["sent"]]).start()
            done["sent"] += 1

    def receive(until, last=None):
        while done["here"] < until:
            item(*items[done["here"]]).wait_recv()
            done["here"] += 1
            push(min(done["here"] + AHEAD, last or len(items)))

    for copy in across:
        copy.wait()
    beside = [remote(windows.at[k], windows.at[k + 1], win_send.at[k + 1], win_recv.at[k + 1], me ^ 1) for k in (0, 2, 4, 6)]
    for copy in beside:
        copy.start()

    def collect(*arrays):
        def copies(k, buffer):
            begin = 0
            for n, a in enumerate(arrays):
                src = stage.at[buffer, :, pl.ds(begin, widths[a])]
                begin += widths[a]
                yield pltpu.make_async_copy(src, sent[a].at[k], stage_sems.at[2 * n + buffer])

        def step(n, carry):
            buffer = n & 1

            @pl.when(n >= 2)
            def _():
                for copy in copies(0, buffer):
                    copy.wait()

            gather(n ^ 6, buffer)
            for copy in copies(n ^ 6, buffer):
                copy.start()
            return carry

        lax.fori_loop(0, PEERS, step, 0)
        for buffer in range(2):
            for copy in copies(0, buffer):
                copy.wait()

    loads[1].wait()
    spread_out(rows.at[1], spread)
    collect(1)
    push(AHEAD)

    for copy in beside:
        copy.wait()
    for k in range(PEERS):
        for m in range(2):
            wide[m, k * A_DEV : (k + 1) * A_DEV, :] = windows[k, m * A_DEV : (m + 1) * A_DEV, :]
    group = part.shape[2]

    def cost(j, carry):
        at = pl.ds(pl.multiple_of(j * COST_ROWS, COST_ROWS), COST_ROWS)
        both = [
            lax.dot_general(wide[m], rows[m, at, :], OVER_LANES, preferred_element_type=jnp.float32) for m in range(2)
        ]
        value = both[0] + both[1]
        for k in range(PEERS):
            for c in range(cols):
                begin = k * A_DEV + c * group
                part[c, me ^ k, :, at] = value[begin : begin + group]
        return carry

    lax.fori_loop(0, count // COST_ROWS, cost, 0)
    exchanged = [
        remote(part.at[column ^ k], shares.at[k - 1], share_send.at[k], share_recv.at[k], column ^ k, "cols")
        for k in range(1, cols)
    ]
    for copy in exchanged:
        copy.start()
    load = pltpu.make_async_copy(down_b, rows.at[0], load_sems.at[0])
    load.start()
    load.wait()
    spread_out(rows.at[0], spread)
    collect(2, 3)

    def place(a, initial, out):
        width = widths[a]
        tiles = width // LANES
        lanes = pl.ds(0, width)
        table[...] = first_of(slot[...], tiles)
        to_table = pltpu.make_async_copy(table, begins, own_sem)
        to_table.start()
        ours = pltpu.make_async_copy(initial.at[:, lanes], rows.at[1, :, lanes], load_sems.at[1])
        ours.start()
        own_rows = pltpu.make_async_copy(sent[a].at[0], rows.at[0, pl.ds(0, slots), lanes], stage_sems.at[0])
        own_rows.start()
        fetched = [
            pltpu.make_async_copy(moved[a].at[k], rows.at[0, pl.ds(k * slots, slots), lanes], strip_sems.at[k])
            for k in range(1, PEERS)
        ]
        for copy in fetched:
            copy.start()
        own_rows.wait()
        for copy in fetched:
            copy.wait()
        spread_out(rows.at[0], spread, tiles)
        to_table.wait()
        ours.wait()
        read = table_reader(begins)

        def step(j, carry):
            for row, c, tile in rows_of(lambda s: read(j, s), spread, turn, tiles):
                at = pl.ds(pl.multiple_of(j * ROWS + row, 16), 16)
                columns = slice(c * LANES, (c + 1) * LANES)
                mean = (rows[1, at, columns].astype(jnp.float32) + tile) * 0.5
                rows[1, at, columns] = mean.astype(jnp.bfloat16)
            return carry

        lax.fori_loop(0, count // ROWS, step, 0)
        written = pltpu.make_async_copy(rows.at[1, :, lanes], out, load_sems.at[1])
        written.start()
        written.wait()

    held_back = 3 * len(ORDER)
    receive(len(ORDER), held_back)
    place(0, up_a, means[0])
    receive(2 * len(ORDER), held_back)
    place(1, gate_a, means[1])
    for copy in exchanged:
        copy.wait()
    for block in range(PEERS):
        value = part[column, block]
        for k in range(1, cols):
            value = value + shares[k - 1, block]
        value = value * (2.0 * D) ** (-0.5)
        for m in range(group):
            costs_ref[m * PEERS + block : m * PEERS + block + 1, :] = value[m : m + 1]
    receive(held_back - 3, held_back)
    push(len(items))
    receive(held_back)
    place(2, down_a, means[2])
    receive(len(items))
    for a, k in items:
        item(a, k).wait_send()


def last_kernel(cut, begins, up_ref, gate_ref, down_ref, costs_ref, own_ref, moved_ref, initial, *refs):
    up_out, gate_out, down_out, costs_out, rows, ours, spread, turn, sems = refs
    count, features = initial.shape
    slots = count // PEERS
    width = features - cut
    tiles = width // LANES
    left, right = pl.ds(0, cut), pl.ds(cut, width)
    fetched = [pltpu.make_async_copy(own_ref.at[0], rows.at[pl.ds(0, slots)], sems.at[0])]
    fetched += [
        pltpu.make_async_copy(moved_ref.at[k], rows.at[pl.ds(k * slots, slots)], sems.at[k]) for k in range(1, PEERS)
    ]
    fetched.append(pltpu.make_async_copy(initial.at[:, right], ours, sems.at[PEERS]))
    handed = []
    piece = count // PARTS
    for n in range(PARTS):
        at = pl.ds(n * piece, piece)
        pairs = ((up_ref, up_out.at[at]), (gate_ref, gate_out.at[at]), (down_ref, down_out.at[at, left]))
        for m, (src, dst) in enumerate(pairs):
            handed.append(pltpu.make_async_copy(src.at[at], dst, sems.at[PEERS + 1 + 3 * n + m]))
    handed.append(pltpu.make_async_copy(costs_ref, costs_out, sems.at[PEERS + 1 + 3 * PARTS]))
    for copy in fetched + handed:
        copy.start()
    for copy in fetched:
        copy.wait()
    spread_out(rows, spread)
    read = table_reader(begins)

    def step(j, carry):
        for row, c, tile in rows_of(lambda s: read(j, s), spread, turn, tiles):
            at = pl.ds(pl.multiple_of(j * ROWS + row, 16), 16)
            columns = slice(c * LANES, (c + 1) * LANES)
            ours[at, columns] = ((ours[at, columns].astype(jnp.float32) + tile) * 0.5).astype(jnp.bfloat16)
        return carry

    lax.fori_loop(0, count // ROWS, step, 0)
    written = pltpu.make_async_copy(ours, down_out.at[:, right], sems.at[0])
    written.start()
    for copy in handed:
        copy.wait()
    written.wait()


def balanced(up_a, gate_a, down_a, up_b, gate_b, down_b, perm):
    count, features = up_a.shape
    cols = lax.axis_size("cols")
    cut = features * 3 // 4
    used = count // LANES
    pad = -(-used // 8) * 8
    slots = count // PEERS
    lanes = -(-slots // LANES) * LANES
    tiles = features // LANES
    vmem, smem = pl.BlockSpec(memory_space=pltpu.VMEM), pl.BlockSpec(memory_space=pltpu.SMEM)
    hbm = pl.BlockSpec(memory_space=pltpu.HBM)
    bf16, f32, i32 = jnp.bfloat16, jnp.float32, jnp.int32
    group = A_DEV // cols
    whole = jax.ShapeDtypeStruct((count, features), bf16)
    costs_shape = jax.ShapeDtypeStruct((group * PEERS, count), f32)
    lists = [jax.ShapeDtypeStruct((PEERS, slots, size), bf16) for size in (features, features, cut, features - cut)]
    begins, *parts = pl.pallas_call(
        functools.partial(main_kernel, count, cut),
        out_shape=[jax.ShapeDtypeStruct((pad, LANES), i32), whole, whole, jax.ShapeDtypeStruct((count, cut), bf16), costs_shape]
        + lists * 2,
        in_specs=[vmem] + [hbm] * 6,
        out_specs=[vmem] + [hbm] * 3 + [vmem] + [hbm] * 8,
        scratch_shapes=[
            pltpu.VMEM((slots, count), bf16),
            pltpu.VMEM((2 * PEERS, count), bf16),
            pltpu.VMEM((pad, LANES), i32),
            pltpu.VMEM((pad, LANES), i32),
            pltpu.VMEM((pad, LANES), i32),
            pltpu.SMEM((pad, LANES), i32),
            pltpu.VMEM((PEERS, 8, lanes), i32),
            pltpu.VMEM((PEERS, 8, lanes), i32),
            pltpu.SMEM((PEERS, 8, lanes), i32),
            pltpu.VMEM((32 * A_DEV, features), bf16),
            pltpu.VMEM((2 * A_DEV, features), bf16),
            pltpu.VMEM((PEERS, 2 * A_DEV, features), bf16),
            pltpu.VMEM((2, A_DEV * PEERS, features), bf16),
            pltpu.VMEM((2, count, features), bf16),
            pltpu.VMEM(((count + 8) * tiles, LANES), f32),
            pltpu.VMEM(((ROWS + 8) * tiles, LANES), f32),
            pltpu.VMEM((2, slots, features), bf16),
            pltpu.VMEM((cols, PEERS, group, count), f32),
            pltpu.VMEM((cols - 1, PEERS, group, count), f32),
        ]
        + [pltpu.SemaphoreType.DMA((PEERS,))] * 4
        + [pltpu.SemaphoreType.DMA((4, PEERS))] * 2
        + [pltpu.SemaphoreType.DMA((cols,))] * 2
        + [
            pltpu.SemaphoreType.DMA((2 * A_DEV,)),
            pltpu.SemaphoreType.DMA((2,)),
            pltpu.SemaphoreType.DMA((4,)),
            pltpu.SemaphoreType.DMA,
        ],
        compiler_params=pltpu.CompilerParams(
            collective_id=0, has_side_effects=True, vmem_limit_bytes=62 * 1024 * 1024
        ),
    )(perm.reshape(used, LANES), up_a, gate_a, down_a, up_b, gate_b, down_b)
    up_part, gate_part, down_part, costs_part = parts[:4]
    own, moved = parts[7], parts[11]
    width = features - cut
    up_mean, gate_mean, down_mean, costs = pl.pallas_call(
        functools.partial(last_kernel, cut),
        out_shape=[whole, whole, whole, costs_shape],
        in_specs=[smem] + [hbm] * 7,
        out_specs=[hbm] * 4,
        scratch_shapes=[
            pltpu.VMEM((count, width), bf16),
            pltpu.VMEM((count, width), bf16),
            pltpu.VMEM(((count + 8) * width // LANES, LANES), f32),
            pltpu.VMEM(((ROWS + 8) * width // LANES, LANES), f32),
            pltpu.SemaphoreType.DMA((PEERS + 2 + 3 * PARTS,)),
        ],
        compiler_params=pltpu.CompilerParams(vmem_limit_bytes=62 * 1024 * 1024),
    )(begins, up_part, gate_part, down_part, costs_part, own, moved, down_a)
    return (costs.T, up_mean, gate_mean, down_mean)


def pick(array, index):
    rows = jnp.arange(array.shape[0], dtype=jnp.int32)
    hot = (index[:, None] == rows[None, :]).astype(array.dtype)
    return jnp.dot(hot, array, preferred_element_type=jnp.float32).astype(array.dtype)


def mix(initial, picked):
    return ((initial.astype(jnp.float32) + picked.astype(jnp.float32)) * 0.5).astype(jnp.bfloat16)


def general(up_a, gate_a, down_a, up_b, gate_b, down_b, perm):
    row_count, features = up_a.shape
    stride = row_count // A_DEV
    cost_scale = (2.0 * D) ** (-0.5)
    peers = lax.axis_size("rows")
    cols = lax.axis_size("cols")
    capacity = max(2, (row_count + peers - 1) // peers)

    source = perm // row_count
    local_row = perm % row_count
    blocks = jnp.arange(peers, dtype=jnp.int32)
    matches = (source[None, :] == blocks[:, None]).astype(jnp.int32)
    order = jnp.arange(row_count, dtype=jnp.int32)
    ahead = jnp.dot(
        matches.astype(jnp.bfloat16),
        (order[:, None] < order[None, :]).astype(jnp.bfloat16),
        preferred_element_type=jnp.float32,
    )
    arrival_rank = jnp.sum(ahead.astype(jnp.int32) * matches, axis=0)
    high = (local_row // 256).astype(jnp.bfloat16)
    low = (local_row % 256).astype(jnp.bfloat16)
    halves = jnp.stack([high, low])[:, None, :] * matches.astype(jnp.bfloat16)[None]
    at_rank = (arrival_rank[None, :] == jnp.arange(capacity, dtype=jnp.int32)[:, None]).astype(jnp.bfloat16)
    found = jnp.einsum("hsi,ri->hsr", halves, at_rank, preferred_element_type=jnp.float32)
    wanted = found[0].astype(jnp.int32) * 256 + found[1].astype(jnp.int32)
    asked = lax.all_to_all(wanted, "rows", split_axis=0, concat_axis=0, tiled=True).reshape(-1)
    slot = source * capacity + arrival_rank

    window = jnp.concatenate([up_a[::stride], gate_a[::stride]], axis=0)
    pieces = lax.all_gather(window, "rows").reshape(peers, 2, A_DEV, features)
    wide = pieces.transpose(1, 2, 0, 3).reshape(2, A_DEV * peers, features)
    partial_value = jnp.einsum("kd,jd->kj", wide[0], up_b, preferred_element_type=jnp.float32)
    partial_value = partial_value + jnp.einsum("kd,jd->kj", wide[1], gate_b, preferred_element_type=jnp.float32)
    total = lax.psum_scatter(partial_value.reshape(cols, -1, row_count), "cols", scatter_dimension=0)

    def averaged(initial, other):
        moved = pick(other, asked).reshape(peers, capacity, features)
        moved = lax.all_to_all(moved, "rows", split_axis=0, concat_axis=0, tiled=True)
        return mix(initial, pick(moved.reshape(-1, features), slot))

    return (
        (total * cost_scale).T,
        averaged(up_a, up_b),
        averaged(gate_a, gate_b),
        averaged(down_a, down_b),
    )


def solution(mesh):
    def local(up_a, *rest):
        row_count, features = up_a.shape
        even = mesh.shape["rows"] == PEERS and row_count % (PEERS * 16) == 0 and row_count % (A_DEV * 16) == 0
        even = even and row_count % COST_ROWS == 0 and row_count % (16 * PARTS) == 0 and row_count % (PEERS * ROWS) == 0
        even = even and features == 8 * LANES and mesh.shape["cols"] == A_DEV // 8
        return (balanced if even else general)(up_a, *rest)

    placed = (P("rows", "cols"),) * 6 + (P("rows"),)
    return jax.shard_map(
        local,
        mesh=mesh,
        in_specs=placed,
        out_specs=(P("rows", "cols"),) * 4,
        check_vma=False,
    )
```

```python
import functools

import jax
import jax.numpy as jnp
from jax import lax
from jax.experimental import pallas as pl
from jax.experimental.pallas import tpu as pltpu
from jax.sharding import PartitionSpec as P

D = 4096
A_DEV = 32
MESH = pl.DeviceIdType.MESH

PEERS = 8
LANES = 128
ORDER = (6, 7, 4, 5, 2, 3, 1)
LATER = (2, 4, 3, 5, 1, 6, 7)
AHEAD = 9
ROWS = 32
COST_ROWS = 512
PARTS = 4
OVER_LANES = (((1,), (1,)), ((), ()))


def one_hot(hit):
    return jnp.where(hit, 1.0, 0.0).astype(jnp.bfloat16)


def matmul(a, b):
    return jnp.dot(a, b, preferred_element_type=jnp.float32)


def count_ranks(count, me, perm_ref, slot_ref, hot, halves, padded, sent):
    used, pad = perm_ref.shape[0], padded.shape[0]
    slots = count // PEERS
    padded[...] = jnp.full(padded.shape, PEERS * count, jnp.int32)
    padded[:used] = perm_ref[...]
    perm = padded[...]
    source = jnp.zeros_like(perm)
    for k in range(1, PEERS + 1):
        source = source + jnp.where(perm >= k * count, 1, 0)
    row = perm - source * count
    masks = jnp.concatenate([jnp.where(source == k, 1.0, 0.0) for k in range(PEERS)], axis=0)
    packed = masks.astype(jnp.bfloat16)
    shape = (LANES, LANES)
    lane_before = one_hot(lax.broadcasted_iota(jnp.int32, shape, 0) < lax.broadcasted_iota(jnp.int32, shape, 1))
    within = matmul(packed, lane_before)
    totals = matmul(packed, jnp.ones(shape, jnp.bfloat16)).astype(jnp.bfloat16)
    shape = (PEERS * pad, PEERS * pad)
    left, right = lax.broadcasted_iota(jnp.int32, shape, 0), lax.broadcasted_iota(jnp.int32, shape, 1)
    row_before = one_hot((right < left) & (right >= left - lax.rem(left, pad)))
    ahead = matmul(row_before, totals)
    ranked = masks * (within + ahead)
    rank = ranked[:pad]
    for k in range(1, PEERS):
        rank = rank + ranked[k * pad : (k + 1) * pad]
    rank = rank.astype(jnp.int32)
    slot_ref[...] = jnp.clip((source ^ me) * slots + rank, 0, count - 1)

    high = lax.shift_right_logical(row, 8).astype(jnp.float32)
    low = (row & 255).astype(jnp.float32)
    block = lax.broadcasted_iota(jnp.int32, (PEERS, LANES), 0)
    slot = lax.broadcasted_iota(jnp.int32, (slots, LANES), 0)
    for j in range(used):
        at = slice(j * LANES, (j + 1) * LANES)
        one = slice(j, j + 1)
        mine = source[one] == block
        both = [jnp.where(mine, part[one], 0.0) for part in (high, low)]
        halves[:, at] = jnp.concatenate(both, axis=0).astype(jnp.bfloat16)
        hot[:, at] = one_hot(rank[one] == slot)
    found = lax.dot_general(halves[...], hot[...], OVER_LANES, preferred_element_type=jnp.float32)
    wanted = found[:PEERS] * 256.0 + found[PEERS:]
    for k in range(PEERS):
        sent[k, :, :slots] = jnp.broadcast_to(wanted[k : k + 1], (8, slots)).astype(jnp.int32)
        sent[k, :, slots:] = jnp.zeros((8, sent.shape[2] - slots), jnp.int32)


def spread_out(rows_ref, spread, tiles=None):
    tall, width = rows_ref.shape
    tiles = tiles or width // LANES

    def step(m, carry):
        for c in range(tiles):
            v = rows_ref[pl.ds(pl.multiple_of(m * 16, 16), 16), c * LANES : (c + 1) * LANES].astype(jnp.float32)
            for h in range(2):
                to = (m * 2 + h) * 8 * tiles + c * 8
                spread[pl.ds(pl.multiple_of(to, 8), 8), :] = v[h * 8 : h * 8 + 8]
        return carry

    lax.fori_loop(0, tall // 16, step, 0)


def first_of(row, tiles):
    return lax.shift_right_logical(row, 3) * (8 * tiles) + (row & 7)


def rows_of(begin_of, spread, turn, tiles):
    for s in range(ROWS):
        to = (s // 8) * 8 * tiles + s % 8
        turn[pl.ds(to, tiles, stride=8), :] = spread[pl.ds(begin_of(s), tiles, stride=8), :]
    for h in range(ROWS // 16):
        for c in range(tiles):
            both = [turn[pl.ds(((2 * h + half) * tiles + c) * 8, 8), :] for half in range(2)]
            yield h * 16, c, jnp.concatenate(both, axis=0)


def table_reader(table):
    per = LANES // ROWS

    def read(j, s):
        return table[lax.div(j, per), lax.rem(j, per) * ROWS + s]

    return read


def main_kernel(count, cut, perm_ref, up_a, gate_a, down_a, up_b, gate_b, down_b, *refs):
    begin_ref, means, costs_ref, refs = refs[0], refs[1:4], refs[4], refs[5:]
    sent, moved, refs = refs[:4], refs[4:8], refs[8:]
    hot, halves, padded, slot, table, begins, ask, got, asked, held, window, windows, wide, rows, spread, turn, stage = refs[:17]
    part, shares, refs = refs[17], refs[18], refs[19:]
    ask_send, ask_recv, win_send, win_recv, item_send, item_recv, share_send, share_recv, strip_sems, load_sems, stage_sems, own_sem = refs
    me, column = lax.axis_index("rows"), lax.axis_index("cols")
    slots = count // PEERS
    stride = count // A_DEV
    cols = part.shape[0]
    features = up_a.shape[1]
    widths = (features, features, cut, features - cut)
    barrier = pltpu.get_barrier_semaphore()
    for k in range(1, PEERS):
        pl.semaphore_signal(barrier, inc=1, device_id={"rows": me ^ k}, device_id_type=MESH)
    for k in range(1, cols):
        pl.semaphore_signal(barrier, inc=1, device_id={"cols": column ^ k}, device_id_type=MESH)

    strips = []
    for m, ref in enumerate((up_a, gate_a)):
        for i in range(A_DEV):
            at = m * A_DEV + i
            strips.append(
                pltpu.make_async_copy(ref.at[pl.ds(i * stride, 16)], held.at[pl.ds(at * 16, 16)], strip_sems.at[at])
            )
    for copy in strips:
        copy.start()
    loads = [pltpu.make_async_copy(ref, rows.at[n], load_sems.at[n]) for n, ref in enumerate((up_b, gate_b))]
    for copy in loads:
        copy.start()

    for copy in strips:
        copy.wait()
    shape = (2 * A_DEV, 32 * A_DEV)
    first = lax.broadcasted_iota(jnp.int32, shape, 0) * 16 == lax.broadcasted_iota(jnp.int32, shape, 1)
    window[...] = matmul(one_hot(first), held[...]).astype(jnp.bfloat16)
    windows[0] = window[...]
    pl.semaphore_wait(barrier, PEERS - 1 + cols - 1)

    def remote(src, dst, send, recv, peer, axis="rows"):
        return pltpu.make_async_remote_copy(
            src_ref=src, dst_ref=dst, send_sem=send, recv_sem=recv, device_id={axis: peer}, device_id_type=MESH
        )

    across = [remote(window, windows.at[k], win_send.at[k], win_recv.at[k], me ^ k) for k in (6, 2, 4)]
    for copy in across:
        copy.start()

    count_ranks(count, me, perm_ref, slot, hot, halves, padded, ask)
    asks = [remote(ask.at[me ^ k], got.at[k], ask_send.at[k], ask_recv.at[k], me ^ k) for k in ORDER]
    for copy in asks:
        copy.start()
    own = pltpu.make_async_copy(ask.at[me], got.at[0], own_sem)
    own.start()
    begin_ref[...] = first_of(slot[...], widths[3] // LANES)
    loads[0].wait()
    spread_out(rows.at[0], spread)
    own.wait()
    for copy in asks:
        copy.wait()
    got[...] = first_of(jnp.clip(got[...], 0, count - 1), features // LANES)
    own = pltpu.make_async_copy(got, asked, own_sem)
    own.start()
    own.wait()

    def gather(k, buffer):
        def step(t, carry):
            for row, c, tile in rows_of(lambda s: asked[k, 0, t * ROWS + s], spread, turn, features // LANES):
                at = pl.ds(pl.multiple_of(t * ROWS + row, 16), 16)
                stage[buffer, at, c * LANES : (c + 1) * LANES] = tile.astype(jnp.bfloat16)
            return carry

        lax.fori_loop(0, slots // ROWS, step, 0)

    items = [(a, k) for a in range(4) for k in (ORDER if a < 2 else LATER)]

    def item(a, k):
        return remote(sent[a].at[k], moved[a].at[k], item_send.at[a, k], item_recv.at[a, k], me ^ k)

    def up_step(n, carry):
        k = n ^ 6
        gather(k, 0)
        copy = pltpu.make_async_copy(stage.at[0], sent[0].at[k], stage_sems.at[0])
        copy.start()
        copy.wait()

        @pl.when(k > 0)
        def _():
            item(0, k).start()

        return carry

    lax.fori_loop(0, PEERS, up_step, 0)
    done = {"sent": len(ORDER), "here": 0}

    def push(count_of):
        while done["sent"] < count_of:
            item(*items[done["sent"]]).start()
            done["sent"] += 1

    def receive(until, last=None):
        while done["here"] < until:
            item(*items[done["here"]]).wait_recv()
            done["here"] += 1
            push(min(done["here"] + AHEAD, last or len(items)))

    for copy in across:
        copy.wait()
    beside = [remote(windows.at[k], windows.at[k + 1], win_send.at[k + 1], win_recv.at[k + 1], me ^ 1) for k in (0, 2, 4, 6)]
    for copy in beside:
        copy.start()

    def collect(*arrays):
        def copies(k, buffer):
            begin = 0
            for n, a in enumerate(arrays):
                src = stage.at[buffer, :, pl.ds(begin, widths[a])]
                begin += widths[a]
                yield pltpu.make_async_copy(src, sent[a].at[k], stage_sems.at[2 * n + buffer])

        def step(n, carry):
            buffer = n & 1

            @pl.when(n >= 2)
            def _():
                for copy in copies(0, buffer):
                    copy.wait()

            gather(n ^ 6, buffer)
            for copy in copies(n ^ 6, buffer):
                copy.start()
            return carry

        lax.fori_loop(0, PEERS, step, 0)
        for buffer in range(2):
            for copy in copies(0, buffer):
                copy.wait()

    loads[1].wait()
    spread_out(rows.at[1], spread)
    collect(1)
    push(AHEAD)

    for copy in beside:
        copy.wait()
    for k in range(PEERS):
        for m in range(2):
            wide[m, k * A_DEV : (k + 1) * A_DEV, :] = windows[k, m * A_DEV : (m + 1) * A_DEV, :]
    group = part.shape[2]

    def cost(j, carry):
        at = pl.ds(pl.multiple_of(j * COST_ROWS, COST_ROWS), COST_ROWS)
        both = [
            lax.dot_general(wide[m], rows[m, at, :], OVER_LANES, preferred_element_type=jnp.float32) for m in range(2)
        ]
        value = both[0] + both[1]
        for k in range(PEERS):
            for c in range(cols):
                begin = k * A_DEV + c * group
                part[c, me ^ k, :, at] = value[begin : begin + group]
        return carry

    lax.fori_loop(0, count // COST_ROWS, cost, 0)
    exchanged = [
        remote(part.at[column ^ k], shares.at[k - 1], share_send.at[k], share_recv.at[k], column ^ k, "cols")
        for k in range(1, cols)
    ]
    for copy in exchanged:
        copy.start()
    load = pltpu.make_async_copy(down_b, rows.at[0], load_sems.at[0])
    load.start()
    load.wait()
    spread_out(rows.at[0], spread)
    collect(2, 3)

    def place(a, initial, out):
        width = widths[a]
        tiles = width // LANES
        lanes = pl.ds(0, width)
        table[...] = first_of(slot[...], tiles)
        to_table = pltpu.make_async_copy(table, begins, own_sem)
        to_table.start()
        ours = pltpu.make_async_copy(initial.at[:, lanes], rows.at[1, :, lanes], load_sems.at[1])
        ours.start()
        own_rows = pltpu.make_async_copy(sent[a].at[0], rows.at[0, pl.ds(0, slots), lanes], stage_sems.at[0])
        own_rows.start()
        fetched = [
            pltpu.make_async_copy(moved[a].at[k], rows.at[0, pl.ds(k * slots, slots), lanes], strip_sems.at[k])
            for k in range(1, PEERS)
        ]
        for copy in fetched:
            copy.start()
        own_rows.wait()
        for copy in fetched:
            copy.wait()
        spread_out(rows.at[0], spread, tiles)
        to_table.wait()
        ours.wait()
        read = table_reader(begins)

        def step(j, carry):
            for row, c, tile in rows_of(lambda s: read(j, s), spread, turn, tiles):
                at = pl.ds(pl.multiple_of(j * ROWS + row, 16), 16)
                columns = slice(c * LANES, (c + 1) * LANES)
                mean = (rows[1, at, columns].astype(jnp.float32) + tile) * 0.5
                rows[1, at, columns] = mean.astype(jnp.bfloat16)
            return carry

        lax.fori_loop(0, count // ROWS, step, 0)
        written = pltpu.make_async_copy(rows.at[1, :, lanes], out, load_sems.at[1])
        written.start()
        written.wait()

    held_back = 3 * len(ORDER)
    receive(len(ORDER), held_back)
    place(0, up_a, means[0])
    receive(2 * len(ORDER), held_back)
    place(1, gate_a, means[1])
    for copy in exchanged:
        copy.wait()
    for block in range(PEERS):
        value = part[column, block]
        for k in range(1, cols):
            value = value + shares[k - 1, block]
        value = value * (2.0 * D) ** (-0.5)
        for m in range(group):
            costs_ref[m * PEERS + block : m * PEERS + block + 1, :] = value[m : m + 1]
    receive(held_back - 3, held_back)
    push(len(items))
    receive(held_back)
    place(2, down_a, means[2])
    receive(len(items))
    for a, k in items:
        item(a, k).wait_send()


def last_kernel(cut, begins, up_ref, gate_ref, down_ref, costs_ref, own_ref, moved_ref, initial, *refs):
    up_out, gate_out, down_out, costs_out, rows, ours, spread, turn, up, gate, down, costs, sems, in_sems, out_sems = refs
    count, features = initial.shape
    slots = count // PEERS
    width = features - cut
    tiles = width // LANES
    left, right = pl.ds(0, cut), pl.ds(cut, width)
    fetched = [pltpu.make_async_copy(own_ref.at[0], rows.at[pl.ds(0, slots)], sems.at[0])]
    fetched += [
        pltpu.make_async_copy(moved_ref.at[k], rows.at[pl.ds(k * slots, slots)], sems.at[k]) for k in range(1, PEERS)
    ]
    fetched.append(pltpu.make_async_copy(initial.at[:, right], ours, sems.at[PEERS]))
    piece = count // PARTS
    read_in, handed = [], []
    for n in range(PARTS):
        at = pl.ds(n * piece, piece)
        ways = ((up_ref.at[at], up.at[at], up_out.at[at]), (gate_ref.at[at], gate.at[at], gate_out.at[at]))
        ways += ((down_ref.at[at], down.at[at], down_out.at[at, left]),)
        ways += ((costs_ref, costs, costs_out),) if n == 0 else ()
        read_in.append([pltpu.make_async_copy(w[0], w[1], in_sems.at[n, m]) for m, w in enumerate(ways)])
        handed.append([pltpu.make_async_copy(w[1], w[2], out_sems.at[n, m]) for m, w in enumerate(ways)])
    for copy in fetched:
        copy.start()
    for copies in read_in:
        for copy in copies:
            copy.start()
    for copy in fetched:
        copy.wait()
    spread_out(rows, spread)
    read = table_reader(begins)

    def step(j, carry):
        for row, c, tile in rows_of(lambda s: read(j, s), spread, turn, tiles):
            at = pl.ds(pl.multiple_of(j * ROWS + row, 16), 16)
            columns = slice(c * LANES, (c + 1) * LANES)
            ours[at, columns] = ((ours[at, columns].astype(jnp.float32) + tile) * 0.5).astype(jnp.bfloat16)
        return carry

    steps = piece // ROWS
    written = []
    for n in range(PARTS):
        for come, go in zip(read_in[n], handed[n]):
            come.wait()
            go.start()
        lax.fori_loop(n * steps, (n + 1) * steps, step, 0)
        at = pl.ds(n * piece, piece)
        written.append(pltpu.make_async_copy(ours.at[at], down_out.at[at, right], sems.at[n]))
        written[n].start()
    for copies in handed:
        for copy in copies:
            copy.wait()
    for copy in written:
        copy.wait()


def balanced(up_a, gate_a, down_a, up_b, gate_b, down_b, perm):
    count, features = up_a.shape
    cols = lax.axis_size("cols")
    cut = features * 3 // 4
    used = count // LANES
    pad = -(-used // 8) * 8
    slots = count // PEERS
    lanes = -(-slots // LANES) * LANES
    tiles = features // LANES
    vmem, smem = pl.BlockSpec(memory_space=pltpu.VMEM), pl.BlockSpec(memory_space=pltpu.SMEM)
    hbm = pl.BlockSpec(memory_space=pltpu.HBM)
    bf16, f32, i32 = jnp.bfloat16, jnp.float32, jnp.int32
    group = A_DEV // cols
    whole = jax.ShapeDtypeStruct((count, features), bf16)
    costs_shape = jax.ShapeDtypeStruct((group * PEERS, count), f32)
    lists = [jax.ShapeDtypeStruct((PEERS, slots, size), bf16) for size in (features, features, cut, features - cut)]
    begins, *parts = pl.pallas_call(
        functools.partial(main_kernel, count, cut),
        out_shape=[jax.ShapeDtypeStruct((pad, LANES), i32), whole, whole, jax.ShapeDtypeStruct((count, cut), bf16), costs_shape]
        + lists * 2,
        in_specs=[vmem] + [hbm] * 6,
        out_specs=[vmem] + [hbm] * 3 + [vmem] + [hbm] * 8,
        scratch_shapes=[
            pltpu.VMEM((slots, count), bf16),
            pltpu.VMEM((2 * PEERS, count), bf16),
            pltpu.VMEM((pad, LANES), i32),
            pltpu.VMEM((pad, LANES), i32),
            pltpu.VMEM((pad, LANES), i32),
            pltpu.SMEM((pad, LANES), i32),
            pltpu.VMEM((PEERS, 8, lanes), i32),
            pltpu.VMEM((PEERS, 8, lanes), i32),
            pltpu.SMEM((PEERS, 8, lanes), i32),
            pltpu.VMEM((32 * A_DEV, features), bf16),
            pltpu.VMEM((2 * A_DEV, features), bf16),
            pltpu.VMEM((PEERS, 2 * A_DEV, features), bf16),
            pltpu.VMEM((2, A_DEV * PEERS, features), bf16),
            pltpu.VMEM((2, count, features), bf16),
            pltpu.VMEM(((count + 8) * tiles, LANES), f32),
            pltpu.VMEM(((ROWS + 8) * tiles, LANES), f32),
            pltpu.VMEM((2, slots, features), bf16),
            pltpu.VMEM((cols, PEERS, group, count), f32),
            pltpu.VMEM((cols - 1, PEERS, group, count), f32),
        ]
        + [pltpu.SemaphoreType.DMA((PEERS,))] * 4
        + [pltpu.SemaphoreType.DMA((4, PEERS))] * 2
        + [pltpu.SemaphoreType.DMA((cols,))] * 2
        + [
            pltpu.SemaphoreType.DMA((2 * A_DEV,)),
            pltpu.SemaphoreType.DMA((2,)),
            pltpu.SemaphoreType.DMA((4,)),
            pltpu.SemaphoreType.DMA,
        ],
        compiler_params=pltpu.CompilerParams(
            collective_id=0, has_side_effects=True, vmem_limit_bytes=62 * 1024 * 1024
        ),
    )(perm.reshape(used, LANES), up_a, gate_a, down_a, up_b, gate_b, down_b)
    up_part, gate_part, down_part, costs_part = parts[:4]
    own, moved = parts[7], parts[11]
    width = features - cut
    up_mean, gate_mean, down_mean, costs = pl.pallas_call(
        functools.partial(last_kernel, cut),
        out_shape=[whole, whole, whole, costs_shape],
        in_specs=[smem] + [hbm] * 7,
        out_specs=[hbm] * 4,
        scratch_shapes=[
            pltpu.VMEM((count, width), bf16),
            pltpu.VMEM((count, width), bf16),
            pltpu.VMEM(((count + 8) * width // LANES, LANES), f32),
            pltpu.VMEM(((ROWS + 8) * width // LANES, LANES), f32),
            pltpu.VMEM((count, features), bf16),
            pltpu.VMEM((count, features), bf16),
            pltpu.VMEM((count, cut), bf16),
            pltpu.VMEM(costs_shape.shape, f32),
            pltpu.SemaphoreType.DMA((PEERS + 1,)),
            pltpu.SemaphoreType.DMA((PARTS, 4)),
            pltpu.SemaphoreType.DMA((PARTS, 4)),
        ],
        compiler_params=pltpu.CompilerParams(vmem_limit_bytes=62 * 1024 * 1024),
    )(begins, up_part, gate_part, down_part, costs_part, own, moved, down_a)
    return (costs.T, up_mean, gate_mean, down_mean)


def pick(array, index):
    rows = jnp.arange(array.shape[0], dtype=jnp.int32)
    hot = (index[:, None] == rows[None, :]).astype(array.dtype)
    return jnp.dot(hot, array, preferred_element_type=jnp.float32).astype(array.dtype)


def mix(initial, picked):
    return ((initial.astype(jnp.float32) + picked.astype(jnp.float32)) * 0.5).astype(jnp.bfloat16)


def general(up_a, gate_a, down_a, up_b, gate_b, down_b, perm):
    row_count, features = up_a.shape
    stride = row_count // A_DEV
    cost_scale = (2.0 * D) ** (-0.5)
    peers = lax.axis_size("rows")
    cols = lax.axis_size("cols")
    capacity = max(2, (row_count + peers - 1) // peers)

    source = perm // row_count
    local_row = perm % row_count
    blocks = jnp.arange(peers, dtype=jnp.int32)
    matches = (source[None, :] == blocks[:, None]).astype(jnp.int32)
    order = jnp.arange(row_count, dtype=jnp.int32)
    ahead = jnp.dot(
        matches.astype(jnp.bfloat16),
        (order[:, None] < order[None, :]).astype(jnp.bfloat16),
        preferred_element_type=jnp.float32,
    )
    arrival_rank = jnp.sum(ahead.astype(jnp.int32) * matches, axis=0)
    high = (local_row // 256).astype(jnp.bfloat16)
    low = (local_row % 256).astype(jnp.bfloat16)
    halves = jnp.stack([high, low])[:, None, :] * matches.astype(jnp.bfloat16)[None]
    at_rank = (arrival_rank[None, :] == jnp.arange(capacity, dtype=jnp.int32)[:, None]).astype(jnp.bfloat16)
    found = jnp.einsum("hsi,ri->hsr", halves, at_rank, preferred_element_type=jnp.float32)
    wanted = found[0].astype(jnp.int32) * 256 + found[1].astype(jnp.int32)
    asked = lax.all_to_all(wanted, "rows", split_axis=0, concat_axis=0, tiled=True).reshape(-1)
    slot = source * capacity + arrival_rank

    window = jnp.concatenate([up_a[::stride], gate_a[::stride]], axis=0)
    pieces = lax.all_gather(window, "rows").reshape(peers, 2, A_DEV, features)
    wide = pieces.transpose(1, 2, 0, 3).reshape(2, A_DEV * peers, features)
    partial_value = jnp.einsum("kd,jd->kj", wide[0], up_b, preferred_element_type=jnp.float32)
    partial_value = partial_value + jnp.einsum("kd,jd->kj", wide[1], gate_b, preferred_element_type=jnp.float32)
    total = lax.psum_scatter(partial_value.reshape(cols, -1, row_count), "cols", scatter_dimension=0)

    def averaged(initial, other):
        moved = pick(other, asked).reshape(peers, capacity, features)
        moved = lax.all_to_all(moved, "rows", split_axis=0, concat_axis=0, tiled=True)
        return mix(initial, pick(moved.reshape(-1, features), slot))

    return (
        (total * cost_scale).T,
        averaged(up_a, up_b),
        averaged(gate_a, gate_b),
        averaged(down_a, down_b),
    )


def solution(mesh):
    def local(up_a, *rest):
        row_count, features = up_a.shape
        even = mesh.shape["rows"] == PEERS and row_count % (PEERS * 16) == 0 and row_count % (A_DEV * 16) == 0
        even = even and row_count % COST_ROWS == 0 and row_count % (ROWS * PARTS) == 0 and row_count % (PEERS * ROWS) == 0
        even = even and features == 8 * LANES and mesh.shape["cols"] == A_DEV // 8
        return (balanced if even else general)(up_a, *rest)

    placed = (P("rows", "cols"),) * 6 + (P("rows"),)
    return jax.shard_map(
        local,
        mesh=mesh,
        in_specs=placed,
        out_specs=(P("rows", "cols"),) * 4,
        check_vma=False,
    )
```

```python
import functools

import jax
import jax.numpy as jnp
from jax import lax
from jax.experimental import pallas as pl
from jax.experimental.pallas import tpu as pltpu
from jax.sharding import PartitionSpec as P

D = 4096
A_DEV = 32
MESH = pl.DeviceIdType.MESH

PEERS = 8
LANES = 128
ORDER = (6, 7, 4, 5, 2, 3, 1)
LATER = (2, 4, 3, 5, 1, 6, 7)
AHEAD = 9
ROWS = 32
COST_ROWS = 512
PARTS = 4
OVER_LANES = (((1,), (1,)), ((), ()))


def one_hot(hit):
    return jnp.where(hit, 1.0, 0.0).astype(jnp.bfloat16)


def matmul(a, b):
    return jnp.dot(a, b, preferred_element_type=jnp.float32)


def count_ranks(count, me, perm_ref, slot_ref, hot, halves, padded, sent):
    used, pad = perm_ref.shape[0], padded.shape[0]
    slots = count // PEERS
    padded[...] = jnp.full(padded.shape, PEERS * count, jnp.int32)
    padded[:used] = perm_ref[...]
    perm = padded[...]
    source = jnp.zeros_like(perm)
    for k in range(1, PEERS + 1):
        source = source + jnp.where(perm >= k * count, 1, 0)
    row = perm - source * count
    masks = jnp.concatenate([jnp.where(source == k, 1.0, 0.0) for k in range(PEERS)], axis=0)
    packed = masks.astype(jnp.bfloat16)
    shape = (LANES, LANES)
    lane_before = one_hot(lax.broadcasted_iota(jnp.int32, shape, 0) < lax.broadcasted_iota(jnp.int32, shape, 1))
    within = matmul(packed, lane_before)
    totals = matmul(packed, jnp.ones(shape, jnp.bfloat16)).astype(jnp.bfloat16)
    shape = (PEERS * pad, PEERS * pad)
    left, right = lax.broadcasted_iota(jnp.int32, shape, 0), lax.broadcasted_iota(jnp.int32, shape, 1)
    row_before = one_hot((right < left) & (right >= left - lax.rem(left, pad)))
    ahead = matmul(row_before, totals)
    ranked = masks * (within + ahead)
    rank = ranked[:pad]
    for k in range(1, PEERS):
        rank = rank + ranked[k * pad : (k + 1) * pad]
    rank = rank.astype(jnp.int32)
    slot_ref[...] = jnp.clip((source ^ me) * slots + rank, 0, count - 1)

    high = lax.shift_right_logical(row, 8).astype(jnp.float32)
    low = (row & 255).astype(jnp.float32)
    block = lax.broadcasted_iota(jnp.int32, (PEERS, LANES), 0)
    slot = lax.broadcasted_iota(jnp.int32, (slots, LANES), 0)
    for j in range(used):
        at = slice(j * LANES, (j + 1) * LANES)
        one = slice(j, j + 1)
        mine = source[one] == block
        both = [jnp.where(mine, part[one], 0.0) for part in (high, low)]
        halves[:, at] = jnp.concatenate(both, axis=0).astype(jnp.bfloat16)
        hot[:, at] = one_hot(rank[one] == slot)
    found = lax.dot_general(halves[...], hot[...], OVER_LANES, preferred_element_type=jnp.float32)
    wanted = found[:PEERS] * 256.0 + found[PEERS:]
    for k in range(PEERS):
        sent[k, :, :slots] = jnp.broadcast_to(wanted[k : k + 1], (8, slots)).astype(jnp.int32)
        sent[k, :, slots:] = jnp.zeros((8, sent.shape[2] - slots), jnp.int32)


def spread_out(rows_ref, spread, tiles=None):
    tall, width = rows_ref.shape
    tiles = tiles or width // LANES

    def step(m, carry):
        for c in range(tiles):
            v = rows_ref[pl.ds(pl.multiple_of(m * 16, 16), 16), c * LANES : (c + 1) * LANES].astype(jnp.float32)
            for h in range(2):
                to = (m * 2 + h) * 8 * tiles + c * 8
                spread[pl.ds(pl.multiple_of(to, 8), 8), :] = v[h * 8 : h * 8 + 8]
        return carry

    lax.fori_loop(0, tall // 16, step, 0)


def first_of(row, tiles):
    return lax.shift_right_logical(row, 3) * (8 * tiles) + (row & 7)


def rows_of(begin_of, spread, turn, tiles):
    for s in range(ROWS):
        to = (s // 8) * 8 * tiles + s % 8
        turn[pl.ds(to, tiles, stride=8), :] = spread[pl.ds(begin_of(s), tiles, stride=8), :]
    for h in range(ROWS // 16):
        for c in range(tiles):
            both = [turn[pl.ds(((2 * h + half) * tiles + c) * 8, 8), :] for half in range(2)]
            yield h * 16, c, jnp.concatenate(both, axis=0)


def table_reader(table):
    per = LANES // ROWS

    def read(j, s):
        return table[lax.div(j, per), lax.rem(j, per) * ROWS + s]

    return read


def main_kernel(count, cut, perm_ref, up_a, gate_a, down_a, up_b, gate_b, down_b, *refs):
    begin_ref, means, costs_ref, refs = refs[0], refs[1:4], refs[4], refs[5:]
    sent, moved, refs = refs[:4], refs[4:8], refs[8:]
    hot, halves, padded, slot, table, begins, ask, got, asked, held, window, windows, wide, rows, spread, turn, stage = refs[:17]
    part, shares, refs = refs[17], refs[18], refs[19:]
    ask_send, ask_recv, win_send, win_recv, item_send, item_recv, share_send, share_recv, strip_sems, load_sems, stage_sems, own_sem = refs
    me, column = lax.axis_index("rows"), lax.axis_index("cols")
    slots = count // PEERS
    stride = count // A_DEV
    cols = part.shape[0]
    features = up_a.shape[1]
    widths = (features, features, cut, features - cut)
    barrier = pltpu.get_barrier_semaphore()
    for k in range(1, PEERS):
        pl.semaphore_signal(barrier, inc=1, device_id={"rows": me ^ k}, device_id_type=MESH)
    for k in range(1, cols):
        pl.semaphore_signal(barrier, inc=1, device_id={"cols": column ^ k}, device_id_type=MESH)

    strips = []
    for m, ref in enumerate((up_a, gate_a)):
        for i in range(A_DEV):
            at = m * A_DEV + i
            strips.append(
                pltpu.make_async_copy(ref.at[pl.ds(i * stride, 16)], held.at[pl.ds(at * 16, 16)], strip_sems.at[at])
            )
    for copy in strips:
        copy.start()
    loads = [
        pltpu.make_async_copy(up_b, rows, load_sems.at[0]),
        pltpu.make_async_copy(gate_b, means[1], load_sems.at[1]),
    ]
    for copy in loads:
        copy.start()

    for copy in strips:
        copy.wait()
    shape = (2 * A_DEV, 32 * A_DEV)
    first = lax.broadcasted_iota(jnp.int32, shape, 0) * 16 == lax.broadcasted_iota(jnp.int32, shape, 1)
    window[...] = matmul(one_hot(first), held[...]).astype(jnp.bfloat16)
    windows[0] = window[...]
    pl.semaphore_wait(barrier, PEERS - 1 + cols - 1)

    def remote(src, dst, send, recv, peer, axis="rows"):
        return pltpu.make_async_remote_copy(
            src_ref=src, dst_ref=dst, send_sem=send, recv_sem=recv, device_id={axis: peer}, device_id_type=MESH
        )

    across = [remote(window, windows.at[k], win_send.at[k], win_recv.at[k], me ^ k) for k in (6, 2, 4)]
    for copy in across:
        copy.start()

    count_ranks(count, me, perm_ref, slot, hot, halves, padded, ask)
    asks = [remote(ask.at[me ^ k], got.at[k], ask_send.at[k], ask_recv.at[k], me ^ k) for k in ORDER]
    for copy in asks:
        copy.start()
    own = pltpu.make_async_copy(ask.at[me], got.at[0], own_sem)
    own.start()
    begin_ref[...] = first_of(slot[...], widths[3] // LANES)
    loads[0].wait()
    spread_out(rows, spread)
    own.wait()
    for copy in asks:
        copy.wait()
    got[...] = first_of(jnp.clip(got[...], 0, count - 1), features // LANES)
    own = pltpu.make_async_copy(got, asked, own_sem)
    own.start()
    own.wait()

    def gather(k, buffer):
        def step(t, carry):
            for row, c, tile in rows_of(lambda s: asked[k, 0, t * ROWS + s], spread, turn, features // LANES):
                at = pl.ds(pl.multiple_of(t * ROWS + row, 16), 16)
                stage[buffer, at, c * LANES : (c + 1) * LANES] = tile.astype(jnp.bfloat16)
            return carry

        lax.fori_loop(0, slots // ROWS, step, 0)

    items = [(a, k) for a in range(4) for k in (ORDER if a < 2 else LATER)]

    def item(a, k):
        return remote(sent[a].at[k], moved[a].at[k], item_send.at[a, k], item_recv.at[a, k], me ^ k)

    def up_step(n, carry):
        k = n ^ 6
        gather(k, 0)
        copy = pltpu.make_async_copy(stage.at[0], sent[0].at[k], stage_sems.at[0])
        copy.start()
        copy.wait()

        @pl.when(k > 0)
        def _():
            item(0, k).start()

        return carry

    lax.fori_loop(0, PEERS, up_step, 0)
    done = {"sent": len(ORDER), "here": 0}

    def push(count_of):
        while done["sent"] < count_of:
            item(*items[done["sent"]]).start()
            done["sent"] += 1

    def receive(until, last=None):
        while done["here"] < until:
            item(*items[done["here"]]).wait_recv()
            done["here"] += 1
            push(min(done["here"] + AHEAD, last or len(items)))

    for copy in across:
        copy.wait()
    beside = [remote(windows.at[k], windows.at[k + 1], win_send.at[k + 1], win_recv.at[k + 1], me ^ 1) for k in (0, 2, 4, 6)]
    for copy in beside:
        copy.start()

    def collect(*arrays):
        def copies(k, buffer):
            begin = 0
            for n, a in enumerate(arrays):
                src = stage.at[buffer, :, pl.ds(begin, widths[a])]
                begin += widths[a]
                yield pltpu.make_async_copy(src, sent[a].at[k], stage_sems.at[2 * n + buffer])

        def step(n, carry):
            buffer = n & 1

            @pl.when(n >= 2)
            def _():
                for copy in copies(0, buffer):
                    copy.wait()

            gather(n ^ 6, buffer)
            for copy in copies(n ^ 6, buffer):
                copy.start()
            return carry

        lax.fori_loop(0, PEERS, step, 0)
        for buffer in range(2):
            for copy in copies(0, buffer):
                copy.wait()

    loads[1].wait()
    spread_out(means[1], spread)
    collect(1)
    push(AHEAD)

    for copy in beside:
        copy.wait()
    for k in range(PEERS):
        for m in range(2):
            wide[m, k * A_DEV : (k + 1) * A_DEV, :] = windows[k, m * A_DEV : (m + 1) * A_DEV, :]
    group = part.shape[2]

    def cost(j, carry):
        at = pl.ds(pl.multiple_of(j * COST_ROWS, COST_ROWS), COST_ROWS)
        both = [
            lax.dot_general(wide[m], ref[at, :], OVER_LANES, preferred_element_type=jnp.float32)
            for m, ref in enumerate((rows, means[1]))
        ]
        value = both[0] + both[1]
        for k in range(PEERS):
            for c in range(cols):
                begin = k * A_DEV + c * group
                part[c, me ^ k, :, at] = value[begin : begin + group]
        return carry

    lax.fori_loop(0, count // COST_ROWS, cost, 0)
    exchanged = [
        remote(part.at[column ^ k], shares.at[k - 1], share_send.at[k], share_recv.at[k], column ^ k, "cols")
        for k in range(1, cols)
    ]
    for copy in exchanged:
        copy.start()
    load = pltpu.make_async_copy(down_b, rows, load_sems.at[0])
    load.start()
    load.wait()
    spread_out(rows, spread)
    collect(2, 3)

    def place(a, initial):
        width, out = widths[a], means[a]
        tiles = width // LANES
        lanes = pl.ds(0, width)
        table[...] = first_of(slot[...], tiles)
        to_table = pltpu.make_async_copy(table, begins, own_sem)
        to_table.start()
        ours = pltpu.make_async_copy(initial.at[:, lanes], out, load_sems.at[1])
        ours.start()
        own_rows = pltpu.make_async_copy(sent[a].at[0], rows.at[pl.ds(0, slots), lanes], stage_sems.at[0])
        own_rows.start()
        fetched = [
            pltpu.make_async_copy(moved[a].at[k], rows.at[pl.ds(k * slots, slots), lanes], strip_sems.at[k])
            for k in range(1, PEERS)
        ]
        for copy in fetched:
            copy.start()
        own_rows.wait()
        for copy in fetched:
            copy.wait()
        spread_out(rows, spread, tiles)
        to_table.wait()
        ours.wait()
        read = table_reader(begins)

        def step(j, carry):
            for row, c, tile in rows_of(lambda s: read(j, s), spread, turn, tiles):
                at = pl.ds(pl.multiple_of(j * ROWS + row, 16), 16)
                columns = slice(c * LANES, (c + 1) * LANES)
                out[at, columns] = ((out[at, columns].astype(jnp.float32) + tile) * 0.5).astype(jnp.bfloat16)
            return carry

        lax.fori_loop(0, count // ROWS, step, 0)

    held_back = 3 * len(ORDER)
    receive(len(ORDER), held_back)
    place(0, up_a)
    receive(2 * len(ORDER), held_back)
    place(1, gate_a)
    for copy in exchanged:
        copy.wait()
    for block in range(PEERS):
        value = part[column, block]
        for k in range(1, cols):
            value = value + shares[k - 1, block]
        value = value * (2.0 * D) ** (-0.5)
        for m in range(group):
            costs_ref[m * PEERS + block : m * PEERS + block + 1, :] = value[m : m + 1]
    receive(held_back - 3, held_back)
    push(len(items))
    receive(held_back)
    place(2, down_a)
    receive(len(items))
    for a, k in items:
        item(a, k).wait_send()


def last_kernel(cut, begin_ref, up_ref, gate_ref, down_ref, costs_ref, own_ref, moved_ref, initial, *refs):
    up_out, gate_out, down_out, costs_out, begins, rows, ours, spread, turn, sems, out_sems = refs
    count, features = initial.shape
    slots = count // PEERS
    width = features - cut
    tiles = width // LANES
    left, right = pl.ds(0, cut), pl.ds(cut, width)
    fetched = [pltpu.make_async_copy(own_ref.at[0], rows.at[pl.ds(0, slots)], sems.at[0])]
    fetched += [
        pltpu.make_async_copy(moved_ref.at[k], rows.at[pl.ds(k * slots, slots)], sems.at[k]) for k in range(1, PEERS)
    ]
    fetched.append(pltpu.make_async_copy(initial.at[:, right], ours, sems.at[PEERS]))
    fetched.append(pltpu.make_async_copy(begin_ref, begins, sems.at[PEERS + 1]))
    ways = ((up_ref, up_out), (gate_ref, gate_out), (down_ref, down_out.at[:, left]), (costs_ref, costs_out))
    handed = [pltpu.make_async_copy(src, dst, out_sems.at[n]) for n, (src, dst) in enumerate(ways)]
    for copy in fetched + handed:
        copy.start()
    for copy in fetched:
        copy.wait()
    spread_out(rows, spread)
    read = table_reader(begins)

    def step(j, carry):
        for row, c, tile in rows_of(lambda s: read(j, s), spread, turn, tiles):
            at = pl.ds(pl.multiple_of(j * ROWS + row, 16), 16)
            columns = slice(c * LANES, (c + 1) * LANES)
            ours[at, columns] = ((ours[at, columns].astype(jnp.float32) + tile) * 0.5).astype(jnp.bfloat16)
        return carry

    piece = count // PARTS
    steps = piece // ROWS
    written = []
    for n in range(PARTS):
        lax.fori_loop(n * steps, (n + 1) * steps, step, 0)
        at = pl.ds(n * piece, piece)
        written.append(pltpu.make_async_copy(ours.at[at], down_out.at[at, right], sems.at[n]))
        written[n].start()
    for copy in handed + written:
        copy.wait()


def balanced(up_a, gate_a, down_a, up_b, gate_b, down_b, perm):
    count, features = up_a.shape
    cols = lax.axis_size("cols")
    cut = features * 3 // 4
    used = count // LANES
    pad = -(-used // 8) * 8
    slots = count // PEERS
    lanes = -(-slots // LANES) * LANES
    tiles = features // LANES
    vmem, hbm = pl.BlockSpec(memory_space=pltpu.VMEM), pl.BlockSpec(memory_space=pltpu.HBM)
    bf16, f32, i32 = jnp.bfloat16, jnp.float32, jnp.int32
    group = A_DEV // cols
    whole, kept = jax.ShapeDtypeStruct((count, features), bf16), pltpu.VMEM((count, features), bf16)
    costs_shape = jax.ShapeDtypeStruct((group * PEERS, count), f32)
    lists = [jax.ShapeDtypeStruct((PEERS, slots, size), bf16) for size in (features, features, cut, features - cut)]
    begins, *parts = pl.pallas_call(
        functools.partial(main_kernel, count, cut),
        out_shape=[pltpu.VMEM((pad, LANES), i32), kept, kept, pltpu.VMEM((count, cut), bf16), pltpu.VMEM(costs_shape.shape, f32)]
        + lists * 2,
        in_specs=[vmem] + [hbm] * 6,
        out_specs=[vmem] * 5 + [hbm] * 8,
        scratch_shapes=[
            pltpu.VMEM((slots, count), bf16),
            pltpu.VMEM((2 * PEERS, count), bf16),
            pltpu.VMEM((pad, LANES), i32),
            pltpu.VMEM((pad, LANES), i32),
            pltpu.VMEM((pad, LANES), i32),
            pltpu.SMEM((pad, LANES), i32),
            pltpu.VMEM((PEERS, 8, lanes), i32),
            pltpu.VMEM((PEERS, 8, lanes), i32),
            pltpu.SMEM((PEERS, 8, lanes), i32),
            pltpu.VMEM((32 * A_DEV, features), bf16),
            pltpu.VMEM((2 * A_DEV, features), bf16),
            pltpu.VMEM((PEERS, 2 * A_DEV, features), bf16),
            pltpu.VMEM((2, A_DEV * PEERS, features), bf16),
            pltpu.VMEM((count, features), bf16),
            pltpu.VMEM(((count + 8) * tiles, LANES), f32),
            pltpu.VMEM(((ROWS + 8) * tiles, LANES), f32),
            pltpu.VMEM((2, slots, features), bf16),
            pltpu.VMEM((cols, PEERS, group, count), f32),
            pltpu.VMEM((cols - 1, PEERS, group, count), f32),
        ]
        + [pltpu.SemaphoreType.DMA((PEERS,))] * 4
        + [pltpu.SemaphoreType.DMA((4, PEERS))] * 2
        + [pltpu.SemaphoreType.DMA((cols,))] * 2
        + [
            pltpu.SemaphoreType.DMA((2 * A_DEV,)),
            pltpu.SemaphoreType.DMA((2,)),
            pltpu.SemaphoreType.DMA((4,)),
            pltpu.SemaphoreType.DMA,
        ],
        compiler_params=pltpu.CompilerParams(
            collective_id=0, has_side_effects=True, vmem_limit_bytes=40 * 1024 * 1024
        ),
    )(perm.reshape(used, LANES), up_a, gate_a, down_a, up_b, gate_b, down_b)
    near = [pltpu.with_memory_space_constraint(part, pltpu.VMEM) for part in (begins, *parts[:4])]
    own, moved, initial = (pltpu.with_memory_space_constraint(part, pltpu.HBM) for part in (parts[7], parts[11], down_a))
    width = features - cut
    up_mean, gate_mean, down_mean, costs = pl.pallas_call(
        functools.partial(last_kernel, cut),
        out_shape=[whole, whole, whole, costs_shape],
        in_specs=[vmem] * 5 + [hbm] * 3,
        out_specs=[hbm] * 4,
        scratch_shapes=[
            pltpu.SMEM((pad, LANES), i32),
            pltpu.VMEM((count, width), bf16),
            pltpu.VMEM((count, width), bf16),
            pltpu.VMEM(((count + 8) * width // LANES, LANES), f32),
            pltpu.VMEM(((ROWS + 8) * width // LANES, LANES), f32),
            pltpu.SemaphoreType.DMA((PEERS + 2,)),
            pltpu.SemaphoreType.DMA((4,)),
        ],
        compiler_params=pltpu.CompilerParams(vmem_limit_bytes=12 * 1024 * 1024),
    )(*near, own, moved, initial)
    return (costs.T, up_mean, gate_mean, down_mean)


def pick(array, index):
    rows = jnp.arange(array.shape[0], dtype=jnp.int32)
    hot = (index[:, None] == rows[None, :]).astype(array.dtype)
    return jnp.dot(hot, array, preferred_element_type=jnp.float32).astype(array.dtype)


def mix(initial, picked):
    return ((initial.astype(jnp.float32) + picked.astype(jnp.float32)) * 0.5).astype(jnp.bfloat16)


def general(up_a, gate_a, down_a, up_b, gate_b, down_b, perm):
    row_count, features = up_a.shape
    stride = row_count // A_DEV
    cost_scale = (2.0 * D) ** (-0.5)
    peers = lax.axis_size("rows")
    cols = lax.axis_size("cols")
    capacity = max(2, (row_count + peers - 1) // peers)

    source = perm // row_count
    local_row = perm % row_count
    blocks = jnp.arange(peers, dtype=jnp.int32)
    matches = (source[None, :] == blocks[:, None]).astype(jnp.int32)
    order = jnp.arange(row_count, dtype=jnp.int32)
    ahead = jnp.dot(
        matches.astype(jnp.bfloat16),
        (order[:, None] < order[None, :]).astype(jnp.bfloat16),
        preferred_element_type=jnp.float32,
    )
    arrival_rank = jnp.sum(ahead.astype(jnp.int32) * matches, axis=0)
    high = (local_row // 256).astype(jnp.bfloat16)
    low = (local_row % 256).astype(jnp.bfloat16)
    halves = jnp.stack([high, low])[:, None, :] * matches.astype(jnp.bfloat16)[None]
    at_rank = (arrival_rank[None, :] == jnp.arange(capacity, dtype=jnp.int32)[:, None]).astype(jnp.bfloat16)
    found = jnp.einsum("hsi,ri->hsr", halves, at_rank, preferred_element_type=jnp.float32)
    wanted = found[0].astype(jnp.int32) * 256 + found[1].astype(jnp.int32)
    asked = lax.all_to_all(wanted, "rows", split_axis=0, concat_axis=0, tiled=True).reshape(-1)
    slot = source * capacity + arrival_rank

    window = jnp.concatenate([up_a[::stride], gate_a[::stride]], axis=0)
    pieces = lax.all_gather(window, "rows").reshape(peers, 2, A_DEV, features)
    wide = pieces.transpose(1, 2, 0, 3).reshape(2, A_DEV * peers, features)
    partial_value = jnp.einsum("kd,jd->kj", wide[0], up_b, preferred_element_type=jnp.float32)
    partial_value = partial_value + jnp.einsum("kd,jd->kj", wide[1], gate_b, preferred_element_type=jnp.float32)
    total = lax.psum_scatter(partial_value.reshape(cols, -1, row_count), "cols", scatter_dimension=0)

    def averaged(initial, other):
        moved = pick(other, asked).reshape(peers, capacity, features)
        moved = lax.all_to_all(moved, "rows", split_axis=0, concat_axis=0, tiled=True)
        return mix(initial, pick(moved.reshape(-1, features), slot))

    return (
        (total * cost_scale).T,
        averaged(up_a, up_b),
        averaged(gate_a, gate_b),
        averaged(down_a, down_b),
    )


def solution(mesh):
    def local(up_a, *rest):
        row_count, features = up_a.shape
        even = mesh.shape["rows"] == PEERS and row_count % (PEERS * 16) == 0 and row_count % (A_DEV * 16) == 0
        even = even and row_count % COST_ROWS == 0 and row_count % (ROWS * PARTS) == 0 and row_count % (PEERS * ROWS) == 0
        even = even and features == 8 * LANES and mesh.shape["cols"] == A_DEV // 8
        return (balanced if even else general)(up_a, *rest)

    placed = (P("rows", "cols"),) * 6 + (P("rows"),)
    return jax.shard_map(
        local,
        mesh=mesh,
        in_specs=placed,
        out_specs=(P("rows", "cols"),) * 4,
        check_vma=False,
    )
```

```python
import functools

import jax
import jax.numpy as jnp
from jax import lax
from jax.experimental import pallas as pl
from jax.experimental.pallas import tpu as pltpu
from jax.sharding import PartitionSpec as P

D = 4096
A_DEV = 32
MESH = pl.DeviceIdType.MESH

PEERS = 8
LANES = 128
ORDER = (6, 7, 4, 5, 2, 3, 1)
LATER = (2, 4, 3, 5, 1, 6, 7)
AHEAD = 9
ROWS = 32
COST_ROWS = 512
PARTS = 4
OVER_LANES = (((1,), (1,)), ((), ()))


def one_hot(hit):
    return jnp.where(hit, 1.0, 0.0).astype(jnp.bfloat16)


def matmul(a, b):
    return jnp.dot(a, b, preferred_element_type=jnp.float32)


def count_ranks(count, me, perm_ref, slot_ref, hot, halves, padded, sent):
    used, pad = perm_ref.shape[0], padded.shape[0]
    slots = count // PEERS
    padded[...] = jnp.full(padded.shape, PEERS * count, jnp.int32)
    padded[:used] = perm_ref[...]
    perm = padded[...]
    source = jnp.zeros_like(perm)
    for k in range(1, PEERS + 1):
        source = source + jnp.where(perm >= k * count, 1, 0)
    row = perm - source * count
    masks = jnp.concatenate([jnp.where(source == k, 1.0, 0.0) for k in range(PEERS)], axis=0)
    packed = masks.astype(jnp.bfloat16)
    shape = (LANES, LANES)
    lane_before = one_hot(lax.broadcasted_iota(jnp.int32, shape, 0) < lax.broadcasted_iota(jnp.int32, shape, 1))
    within = matmul(packed, lane_before)
    totals = matmul(packed, jnp.ones(shape, jnp.bfloat16)).astype(jnp.bfloat16)
    shape = (PEERS * pad, PEERS * pad)
    left, right = lax.broadcasted_iota(jnp.int32, shape, 0), lax.broadcasted_iota(jnp.int32, shape, 1)
    row_before = one_hot((right < left) & (right >= left - lax.rem(left, pad)))
    ahead = matmul(row_before, totals)
    ranked = masks * (within + ahead)
    rank = ranked[:pad]
    for k in range(1, PEERS):
        rank = rank + ranked[k * pad : (k + 1) * pad]
    rank = rank.astype(jnp.int32)
    slot_ref[...] = jnp.clip((source ^ me) * slots + rank, 0, count - 1)

    high = lax.shift_right_logical(row, 8).astype(jnp.float32)
    low = (row & 255).astype(jnp.float32)
    block = lax.broadcasted_iota(jnp.int32, (PEERS, LANES), 0)
    slot = lax.broadcasted_iota(jnp.int32, (slots, LANES), 0)
    for j in range(used):
        at = slice(j * LANES, (j + 1) * LANES)
        one = slice(j, j + 1)
        mine = source[one] == block
        both = [jnp.where(mine, part[one], 0.0) for part in (high, low)]
        halves[:, at] = jnp.concatenate(both, axis=0).astype(jnp.bfloat16)
        hot[:, at] = one_hot(rank[one] == slot)
    found = lax.dot_general(halves[...], hot[...], OVER_LANES, preferred_element_type=jnp.float32)
    wanted = found[:PEERS] * 256.0 + found[PEERS:]
    for k in range(PEERS):
        sent[k, :, :slots] = jnp.broadcast_to(wanted[k : k + 1], (8, slots)).astype(jnp.int32)
        sent[k, :, slots:] = jnp.zeros((8, sent.shape[2] - slots), jnp.int32)


def spread_out(rows_ref, spread, tiles=None):
    tall, width = rows_ref.shape
    tiles = tiles or width // LANES

    def step(m, carry):
        for c in range(tiles):
            v = rows_ref[pl.ds(pl.multiple_of(m * 16, 16), 16), c * LANES : (c + 1) * LANES].astype(jnp.float32)
            for h in range(2):
                to = (m * 2 + h) * 8 * tiles + c * 8
                spread[pl.ds(pl.multiple_of(to, 8), 8), :] = v[h * 8 : h * 8 + 8]
        return carry

    lax.fori_loop(0, tall // 16, step, 0)


def first_of(row, tiles):
    return lax.shift_right_logical(row, 3) * (8 * tiles) + (row & 7)


def rows_of(begin_of, spread, turn, tiles):
    for s in range(ROWS):
        to = (s // 8) * 8 * tiles + s % 8
        turn[pl.ds(to, tiles, stride=8), :] = spread[pl.ds(begin_of(s), tiles, stride=8), :]
    for h in range(ROWS // 16):
        for c in range(tiles):
            both = [turn[pl.ds(((2 * h + half) * tiles + c) * 8, 8), :] for half in range(2)]
            yield h * 16, c, jnp.concatenate(both, axis=0)


def paired(begin):
    return begin | lax.shift_left(pltpu.roll(begin, begin.shape[1] - 1, 1), 16)


def half(read, s):
    word = read(s // 2 * 2)
    return lax.shift_right_logical(word, 16) if s % 2 else word & 0xFFFF


def table_reader(table):
    per = LANES // ROWS

    def read(j, s):
        return table[lax.div(j, per), lax.rem(j, per) * ROWS + s]

    return read


def main_kernel(count, cut, perm_ref, up_a, gate_a, down_a, up_b, gate_b, down_b, *refs):
    begin_ref, means, costs_ref, refs = refs[0], refs[1:4], refs[4], refs[5:]
    sent, moved, refs = refs[:4], refs[4:8], refs[8:]
    hot, halves, padded, slot, table, begins, ask, got, asked, held, window, windows, wide, rows, spread, turn, stage = refs[:17]
    part, shares, refs = refs[17], refs[18], refs[19:]
    ask_send, ask_recv, win_send, win_recv, item_send, item_recv, share_send, share_recv, strip_sems, load_sems, stage_sems, own_sem = refs
    me, column = lax.axis_index("rows"), lax.axis_index("cols")
    slots = count // PEERS
    stride = count // A_DEV
    cols = part.shape[0]
    features = up_a.shape[1]
    widths = (features, features, cut, features - cut)
    barrier = pltpu.get_barrier_semaphore()
    for k in range(1, PEERS):
        pl.semaphore_signal(barrier, inc=1, device_id={"rows": me ^ k}, device_id_type=MESH)
    for k in range(1, cols):
        pl.semaphore_signal(barrier, inc=1, device_id={"cols": column ^ k}, device_id_type=MESH)

    strips = []
    for m, ref in enumerate((up_a, gate_a)):
        for i in range(A_DEV):
            at = m * A_DEV + i
            strips.append(
                pltpu.make_async_copy(ref.at[pl.ds(i * stride, 16)], held.at[pl.ds(at * 16, 16)], strip_sems.at[at])
            )
    for copy in strips:
        copy.start()
    loads = [
        pltpu.make_async_copy(up_b, rows, load_sems.at[0]),
        pltpu.make_async_copy(gate_b, means[1], load_sems.at[1]),
    ]
    for copy in loads:
        copy.start()

    def remote(src, dst, send, recv, peer, axis="rows"):
        return pltpu.make_async_remote_copy(
            src_ref=src, dst_ref=dst, send_sem=send, recv_sem=recv, device_id={axis: peer}, device_id_type=MESH
        )

    count_ranks(count, me, perm_ref, slot, hot, halves, padded, ask)
    pl.semaphore_wait(barrier, PEERS - 1 + cols - 1)
    asks = [remote(ask.at[me ^ k], got.at[k], ask_send.at[k], ask_recv.at[k], me ^ k) for k in ORDER]
    for copy in asks:
        copy.start()
    own = pltpu.make_async_copy(ask.at[me], got.at[0], own_sem)
    own.start()
    for copy in strips:
        copy.wait()
    shape = (2 * A_DEV, 32 * A_DEV)
    first = lax.broadcasted_iota(jnp.int32, shape, 0) * 16 == lax.broadcasted_iota(jnp.int32, shape, 1)
    window[...] = matmul(one_hot(first), held[...]).astype(jnp.bfloat16)
    windows[0] = window[...]
    across = [remote(window, windows.at[k], win_send.at[k], win_recv.at[k], me ^ k) for k in (6, 2, 4)]
    for copy in across:
        copy.start()

    begin_ref[...] = first_of(slot[...], widths[3] // LANES)
    loads[0].wait()
    spread_out(rows, spread)
    own.wait()
    for copy in asks:
        copy.wait()
    got[...] = first_of(jnp.clip(got[...], 0, count - 1), features // LANES)
    own = pltpu.make_async_copy(got, asked, own_sem)
    own.start()
    own.wait()

    def gather(k, buffer):
        def step(t, carry):
            for row, c, tile in rows_of(lambda s: asked[k, 0, t * ROWS + s], spread, turn, features // LANES):
                at = pl.ds(pl.multiple_of(t * ROWS + row, 16), 16)
                stage[buffer, at, c * LANES : (c + 1) * LANES] = tile.astype(jnp.bfloat16)
            return carry

        lax.fori_loop(0, slots // ROWS, step, 0)

    items = [(a, k) for a in range(4) for k in (ORDER if a < 2 else LATER)]

    def item(a, k):
        return remote(sent[a].at[k], moved[a].at[k], item_send.at[a, k], item_recv.at[a, k], me ^ k)

    def up_step(n, carry):
        k = n ^ 6
        gather(k, 0)
        copy = pltpu.make_async_copy(stage.at[0], sent[0].at[k], stage_sems.at[0])
        copy.start()
        copy.wait()

        @pl.when(k > 0)
        def _():
            item(0, k).start()

        return carry

    lax.fori_loop(0, PEERS, up_step, 0)
    done = {"sent": len(ORDER), "here": 0}

    def push(count_of):
        while done["sent"] < count_of:
            item(*items[done["sent"]]).start()
            done["sent"] += 1

    def receive(until, last=None):
        while done["here"] < until:
            item(*items[done["here"]]).wait_recv()
            done["here"] += 1
            push(min(done["here"] + AHEAD, last or len(items)))

    for copy in across:
        copy.wait()
    beside = [remote(windows.at[k], windows.at[k + 1], win_send.at[k + 1], win_recv.at[k + 1], me ^ 1) for k in (0, 2, 4, 6)]
    for copy in beside:
        copy.start()

    def collect(*arrays):
        def copies(k, buffer):
            begin = 0
            for n, a in enumerate(arrays):
                src = stage.at[buffer, :, pl.ds(begin, widths[a])]
                begin += widths[a]
                yield pltpu.make_async_copy(src, sent[a].at[k], stage_sems.at[2 * n + buffer])

        def step(n, carry):
            buffer = n & 1

            @pl.when(n >= 2)
            def _():
                for copy in copies(0, buffer):
                    copy.wait()

            gather(n ^ 6, buffer)
            for copy in copies(n ^ 6, buffer):
                copy.start()
            return carry

        lax.fori_loop(0, PEERS, step, 0)
        for buffer in range(2):
            for copy in copies(0, buffer):
                copy.wait()

    loads[1].wait()
    spread_out(means[1], spread)
    collect(1)
    push(AHEAD)

    for copy in beside:
        copy.wait()
    for k in range(PEERS):
        for m in range(2):
            wide[m, k * A_DEV : (k + 1) * A_DEV, :] = windows[k, m * A_DEV : (m + 1) * A_DEV, :]
    group = part.shape[2]

    def cost(j, carry):
        at = pl.ds(pl.multiple_of(j * COST_ROWS, COST_ROWS), COST_ROWS)
        both = [
            lax.dot_general(wide[m], ref[at, :], OVER_LANES, preferred_element_type=jnp.float32)
            for m, ref in enumerate((rows, means[1]))
        ]
        value = both[0] + both[1]
        for k in range(PEERS):
            for c in range(cols):
                begin = k * A_DEV + c * group
                part[c, me ^ k, :, at] = value[begin : begin + group]
        return carry

    lax.fori_loop(0, count // COST_ROWS, cost, 0)
    exchanged = [
        remote(part.at[column ^ k], shares.at[k - 1], share_send.at[k], share_recv.at[k], column ^ k, "cols")
        for k in range(1, cols)
    ]
    for copy in exchanged:
        copy.start()
    load = pltpu.make_async_copy(down_b, rows, load_sems.at[0])
    load.start()
    load.wait()
    spread_out(rows, spread)
    collect(2, 3)

    def place(a, initial):
        width, out = widths[a], means[a]
        tiles = width // LANES
        lanes = pl.ds(0, width)
        table[...] = first_of(slot[...], tiles)
        to_table = pltpu.make_async_copy(table, begins, own_sem)
        to_table.start()
        ours = pltpu.make_async_copy(initial.at[:, lanes], out, load_sems.at[1])
        ours.start()
        own_rows = pltpu.make_async_copy(sent[a].at[0], rows.at[pl.ds(0, slots), lanes], stage_sems.at[0])
        own_rows.start()
        fetched = [
            pltpu.make_async_copy(moved[a].at[k], rows.at[pl.ds(k * slots, slots), lanes], strip_sems.at[k])
            for k in range(1, PEERS)
        ]
        for copy in fetched:
            copy.start()
        own_rows.wait()
        for copy in fetched:
            copy.wait()
        spread_out(rows, spread, tiles)
        to_table.wait()
        ours.wait()
        read = table_reader(begins)

        def step(j, carry):
            for row, c, tile in rows_of(lambda s: read(j, s), spread, turn, tiles):
                at = pl.ds(pl.multiple_of(j * ROWS + row, 16), 16)
                columns = slice(c * LANES, (c + 1) * LANES)
                out[at, columns] = ((out[at, columns].astype(jnp.float32) + tile) * 0.5).astype(jnp.bfloat16)
            return carry

        lax.fori_loop(0, count // ROWS, step, 0)

    held_back = 3 * len(ORDER)
    receive(len(ORDER), held_back)
    place(0, up_a)
    receive(2 * len(ORDER), held_back)
    place(1, gate_a)
    for copy in exchanged:
        copy.wait()
    for block in range(PEERS):
        value = part[column, block]
        for k in range(1, cols):
            value = value + shares[k - 1, block]
        value = value * (2.0 * D) ** (-0.5)
        for m in range(group):
            costs_ref[m * PEERS + block : m * PEERS + block + 1, :] = value[m : m + 1]
    receive(held_back - 3, held_back)
    push(len(items))
    receive(held_back)
    place(2, down_a)
    receive(len(items))
    for a, k in items:
        item(a, k).wait_send()


def last_kernel(cut, begin_ref, up_ref, gate_ref, down_ref, costs_ref, own_ref, moved_ref, initial, *refs):
    up_out, gate_out, down_out, costs_out, table, begins, rows, ours, spread, turn, sems, out_sems = refs
    count, features = initial.shape
    slots = count // PEERS
    width = features - cut
    tiles = width // LANES
    left, right = pl.ds(0, cut), pl.ds(cut, width)
    fetched = [pltpu.make_async_copy(own_ref.at[0], rows.at[pl.ds(0, slots)], sems.at[0])]
    fetched += [
        pltpu.make_async_copy(moved_ref.at[k], rows.at[pl.ds(k * slots, slots)], sems.at[k]) for k in range(1, PEERS)
    ]
    fetched.append(pltpu.make_async_copy(initial.at[:, right], ours, sems.at[PEERS]))
    table[...] = paired(begin_ref[...])
    fetched.append(pltpu.make_async_copy(table, begins, sems.at[PEERS + 1]))
    ways = ((up_ref, up_out), (gate_ref, gate_out), (down_ref, down_out.at[:, left]), (costs_ref, costs_out))
    handed = [pltpu.make_async_copy(src, dst, out_sems.at[n]) for n, (src, dst) in enumerate(ways)]
    for copy in fetched + handed:
        copy.start()
    for copy in fetched:
        copy.wait()
    spread_out(rows, spread)
    read = table_reader(begins)

    def step(j, carry):
        for row, c, tile in rows_of(lambda s: half(lambda even: read(j, even), s), spread, turn, tiles):
            at = pl.ds(pl.multiple_of(j * ROWS + row, 16), 16)
            columns = slice(c * LANES, (c + 1) * LANES)
            ours[at, columns] = ((ours[at, columns].astype(jnp.float32) + tile) * 0.5).astype(jnp.bfloat16)
        return carry

    piece = count // PARTS
    steps = piece // ROWS
    written = []
    for n in range(PARTS):
        lax.fori_loop(n * steps, (n + 1) * steps, step, 0)
        at = pl.ds(n * piece, piece)
        written.append(pltpu.make_async_copy(ours.at[at], down_out.at[at, right], sems.at[n]))
        written[n].start()
    for copy in handed + written:
        copy.wait()


def balanced(up_a, gate_a, down_a, up_b, gate_b, down_b, perm):
    count, features = up_a.shape
    cols = lax.axis_size("cols")
    cut = features * 3 // 4
    used = count // LANES
    pad = -(-used // 8) * 8
    slots = count // PEERS
    lanes = -(-slots // LANES) * LANES
    tiles = features // LANES
    vmem, hbm = pl.BlockSpec(memory_space=pltpu.VMEM), pl.BlockSpec(memory_space=pltpu.HBM)
    bf16, f32, i32 = jnp.bfloat16, jnp.float32, jnp.int32
    group = A_DEV // cols
    whole, kept = jax.ShapeDtypeStruct((count, features), bf16), pltpu.VMEM((count, features), bf16)
    costs_shape = jax.ShapeDtypeStruct((group * PEERS, count), f32)
    lists = [jax.ShapeDtypeStruct((PEERS, slots, size), bf16) for size in (features, features, cut, features - cut)]
    begins, *parts = pl.pallas_call(
        functools.partial(main_kernel, count, cut),
        out_shape=[pltpu.VMEM((pad, LANES), i32), kept, kept, pltpu.VMEM((count, cut), bf16), pltpu.VMEM(costs_shape.shape, f32)]
        + lists * 2,
        in_specs=[vmem] + [hbm] * 6,
        out_specs=[vmem] * 5 + [hbm] * 8,
        scratch_shapes=[
            pltpu.VMEM((slots, count), bf16),
            pltpu.VMEM((2 * PEERS, count), bf16),
            pltpu.VMEM((pad, LANES), i32),
            pltpu.VMEM((pad, LANES), i32),
            pltpu.VMEM((pad, LANES), i32),
            pltpu.SMEM((pad, LANES), i32),
            pltpu.VMEM((PEERS, 8, lanes), i32),
            pltpu.VMEM((PEERS, 8, lanes), i32),
            pltpu.SMEM((PEERS, 8, lanes), i32),
            pltpu.VMEM((32 * A_DEV, features), bf16),
            pltpu.VMEM((2 * A_DEV, features), bf16),
            pltpu.VMEM((PEERS, 2 * A_DEV, features), bf16),
            pltpu.VMEM((2, A_DEV * PEERS, features), bf16),
            pltpu.VMEM((count, features), bf16),
            pltpu.VMEM(((count + 8) * tiles, LANES), f32),
            pltpu.VMEM(((ROWS + 8) * tiles, LANES), f32),
            pltpu.VMEM((2, slots, features), bf16),
            pltpu.VMEM((cols, PEERS, group, count), f32),
            pltpu.VMEM((cols - 1, PEERS, group, count), f32),
        ]
        + [pltpu.SemaphoreType.DMA((PEERS,))] * 4
        + [pltpu.SemaphoreType.DMA((4, PEERS))] * 2
        + [pltpu.SemaphoreType.DMA((cols,))] * 2
        + [
            pltpu.SemaphoreType.DMA((2 * A_DEV,)),
            pltpu.SemaphoreType.DMA((2,)),
            pltpu.SemaphoreType.DMA((4,)),
            pltpu.SemaphoreType.DMA,
        ],
        compiler_params=pltpu.CompilerParams(
            collective_id=0, has_side_effects=True, vmem_limit_bytes=40 * 1024 * 1024
        ),
    )(perm.reshape(used, LANES), up_a, gate_a, down_a, up_b, gate_b, down_b)
    near = [pltpu.with_memory_space_constraint(part, pltpu.VMEM) for part in (begins, *parts[:4])]
    own, moved, initial = (pltpu.with_memory_space_constraint(part, pltpu.HBM) for part in (parts[7], parts[11], down_a))
    width = features - cut
    up_mean, gate_mean, down_mean, costs = pl.pallas_call(
        functools.partial(last_kernel, cut),
        out_shape=[whole, whole, whole, costs_shape],
        in_specs=[vmem] * 5 + [hbm] * 3,
        out_specs=[hbm] * 4,
        scratch_shapes=[
            pltpu.VMEM((pad, LANES), i32),
            pltpu.SMEM((pad, LANES), i32),
            pltpu.VMEM((count, width), bf16),
            pltpu.VMEM((count, width), bf16),
            pltpu.VMEM(((count + 8) * width // LANES, LANES), f32),
            pltpu.VMEM(((ROWS + 8) * width // LANES, LANES), f32),
            pltpu.SemaphoreType.DMA((PEERS + 2,)),
            pltpu.SemaphoreType.DMA((4,)),
        ],
        compiler_params=pltpu.CompilerParams(vmem_limit_bytes=12 * 1024 * 1024),
    )(*near, own, moved, initial)
    return (costs.T, up_mean, gate_mean, down_mean)


def pick(array, index):
    rows = jnp.arange(array.shape[0], dtype=jnp.int32)
    hot = (index[:, None] == rows[None, :]).astype(array.dtype)
    return jnp.dot(hot, array, preferred_element_type=jnp.float32).astype(array.dtype)


def mix(initial, picked):
    return ((initial.astype(jnp.float32) + picked.astype(jnp.float32)) * 0.5).astype(jnp.bfloat16)


def general(up_a, gate_a, down_a, up_b, gate_b, down_b, perm):
    row_count, features = up_a.shape
    stride = row_count // A_DEV
    cost_scale = (2.0 * D) ** (-0.5)
    peers = lax.axis_size("rows")
    cols = lax.axis_size("cols")
    capacity = max(2, (row_count + peers - 1) // peers)

    source = perm // row_count
    local_row = perm % row_count
    blocks = jnp.arange(peers, dtype=jnp.int32)
    matches = (source[None, :] == blocks[:, None]).astype(jnp.int32)
    order = jnp.arange(row_count, dtype=jnp.int32)
    ahead = jnp.dot(
        matches.astype(jnp.bfloat16),
        (order[:, None] < order[None, :]).astype(jnp.bfloat16),
        preferred_element_type=jnp.float32,
    )
    arrival_rank = jnp.sum(ahead.astype(jnp.int32) * matches, axis=0)
    high = (local_row // 256).astype(jnp.bfloat16)
    low = (local_row % 256).astype(jnp.bfloat16)
    halves = jnp.stack([high, low])[:, None, :] * matches.astype(jnp.bfloat16)[None]
    at_rank = (arrival_rank[None, :] == jnp.arange(capacity, dtype=jnp.int32)[:, None]).astype(jnp.bfloat16)
    found = jnp.einsum("hsi,ri->hsr", halves, at_rank, preferred_element_type=jnp.float32)
    wanted = found[0].astype(jnp.int32) * 256 + found[1].astype(jnp.int32)
    asked = lax.all_to_all(wanted, "rows", split_axis=0, concat_axis=0, tiled=True).reshape(-1)
    slot = source * capacity + arrival_rank

    window = jnp.concatenate([up_a[::stride], gate_a[::stride]], axis=0)
    pieces = lax.all_gather(window, "rows").reshape(peers, 2, A_DEV, features)
    wide = pieces.transpose(1, 2, 0, 3).reshape(2, A_DEV * peers, features)
    partial_value = jnp.einsum("kd,jd->kj", wide[0], up_b, preferred_element_type=jnp.float32)
    partial_value = partial_value + jnp.einsum("kd,jd->kj", wide[1], gate_b, preferred_element_type=jnp.float32)
    total = lax.psum_scatter(partial_value.reshape(cols, -1, row_count), "cols", scatter_dimension=0)

    def averaged(initial, other):
        moved = pick(other, asked).reshape(peers, capacity, features)
        moved = lax.all_to_all(moved, "rows", split_axis=0, concat_axis=0, tiled=True)
        return mix(initial, pick(moved.reshape(-1, features), slot))

    return (
        (total * cost_scale).T,
        averaged(up_a, up_b),
        averaged(gate_a, gate_b),
        averaged(down_a, down_b),
    )


def solution(mesh):
    def local(up_a, *rest):
        row_count, features = up_a.shape
        even = mesh.shape["rows"] == PEERS and row_count % (PEERS * 16) == 0 and row_count % (A_DEV * 16) == 0
        even = even and row_count % COST_ROWS == 0 and row_count % (ROWS * PARTS) == 0 and row_count % (PEERS * ROWS) == 0
        even = even and features == 8 * LANES and mesh.shape["cols"] == A_DEV // 8 and row_count * 8 < 2**15
        return (balanced if even else general)(up_a, *rest)

    placed = (P("rows", "cols"),) * 6 + (P("rows"),)
    return jax.shard_map(
        local,
        mesh=mesh,
        in_specs=placed,
        out_specs=(P("rows", "cols"),) * 4,
        check_vma=False,
    )
```

```python
import functools

import jax
import jax.numpy as jnp
from jax import lax
from jax.experimental import pallas as pl
from jax.experimental.pallas import tpu as pltpu
from jax.sharding import PartitionSpec as P

D = 4096
A_DEV = 32
MESH = pl.DeviceIdType.MESH

PEERS = 8
LANES = 128
ORDER = (6, 7, 4, 5, 2, 3, 1)
LATER = (2, 4, 3, 5, 1, 6, 7)
AHEAD = 9
ROWS = 32
COST_ROWS = 512
PARTS = 4
OVER_LANES = (((1,), (1,)), ((), ()))


def one_hot(hit):
    return jnp.where(hit, 1.0, 0.0).astype(jnp.bfloat16)


def matmul(a, b):
    return jnp.dot(a, b, preferred_element_type=jnp.float32)


def count_ranks(count, me, perm_ref, slot_ref, hot, halves, padded, sent):
    used, pad = perm_ref.shape[0], padded.shape[0]
    slots = count // PEERS
    padded[...] = jnp.full(padded.shape, PEERS * count, jnp.int32)
    padded[:used] = perm_ref[...]
    perm = padded[...]
    source = jnp.zeros_like(perm)
    for k in range(1, PEERS + 1):
        source = source + jnp.where(perm >= k * count, 1, 0)
    row = perm - source * count
    masks = jnp.concatenate([jnp.where(source == k, 1.0, 0.0) for k in range(PEERS)], axis=0)
    packed = masks.astype(jnp.bfloat16)
    shape = (LANES, LANES)
    lane_before = one_hot(lax.broadcasted_iota(jnp.int32, shape, 0) < lax.broadcasted_iota(jnp.int32, shape, 1))
    within = matmul(packed, lane_before)
    totals = matmul(packed, jnp.ones(shape, jnp.bfloat16)).astype(jnp.bfloat16)
    shape = (PEERS * pad, PEERS * pad)
    left, right = lax.broadcasted_iota(jnp.int32, shape, 0), lax.broadcasted_iota(jnp.int32, shape, 1)
    row_before = one_hot((right < left) & (right >= left - lax.rem(left, pad)))
    ahead = matmul(row_before, totals)
    ranked = masks * (within + ahead)
    rank = ranked[:pad]
    for k in range(1, PEERS):
        rank = rank + ranked[k * pad : (k + 1) * pad]
    rank = rank.astype(jnp.int32)
    slot_ref[...] = jnp.clip((source ^ me) * slots + rank, 0, count - 1)

    high = lax.shift_right_logical(row, 8).astype(jnp.float32)
    low = (row & 255).astype(jnp.float32)
    block = lax.broadcasted_iota(jnp.int32, (PEERS, LANES), 0)
    slot = lax.broadcasted_iota(jnp.int32, (slots, LANES), 0)
    for j in range(used):
        at = slice(j * LANES, (j + 1) * LANES)
        one = slice(j, j + 1)
        mine = source[one] == block
        both = [jnp.where(mine, part[one], 0.0) for part in (high, low)]
        halves[:, at] = jnp.concatenate(both, axis=0).astype(jnp.bfloat16)
        hot[:, at] = one_hot(rank[one] == slot)
    found = lax.dot_general(halves[...], hot[...], OVER_LANES, preferred_element_type=jnp.float32)
    wanted = found[:PEERS] * 256.0 + found[PEERS:]
    for k in range(PEERS):
        sent[k, :, :slots] = jnp.broadcast_to(wanted[k : k + 1], (8, slots)).astype(jnp.int32)
        sent[k, :, slots:] = jnp.zeros((8, sent.shape[2] - slots), jnp.int32)


def spread_out(rows_ref, spread, tiles=None):
    tall, width = rows_ref.shape
    tiles = tiles or width // LANES

    def step(m, carry):
        for c in range(tiles):
            v = rows_ref[pl.ds(pl.multiple_of(m * 16, 16), 16), c * LANES : (c + 1) * LANES].astype(jnp.float32)
            for h in range(2):
                to = (m * 2 + h) * 8 * tiles + c * 8
                spread[pl.ds(pl.multiple_of(to, 8), 8), :] = v[h * 8 : h * 8 + 8]
        return carry

    lax.fori_loop(0, tall // 16, step, 0)


def first_of(row, tiles):
    return lax.shift_right_logical(row, 3) * (8 * tiles) + (row & 7)


def rows_of(begin_of, spread, turn, tiles):
    for s in range(ROWS):
        to = (s // 8) * 8 * tiles + s % 8
        turn[pl.ds(to, tiles, stride=8), :] = spread[pl.ds(begin_of(s), tiles, stride=8), :]
    for h in range(ROWS // 16):
        for c in range(tiles):
            both = [turn[pl.ds(((2 * h + half) * tiles + c) * 8, 8), :] for half in range(2)]
            yield h * 16, c, jnp.concatenate(both, axis=0)


def paired(begin):
    return begin | lax.shift_left(pltpu.roll(begin, begin.shape[1] - 1, 1), 16)


def half(read, s):
    word = read(s // 2 * 2)
    return lax.shift_right_logical(word, 16) if s % 2 else word & 0xFFFF


def table_reader(table):
    per = LANES // ROWS

    def read(j, s):
        return table[lax.div(j, per), lax.rem(j, per) * ROWS + s]

    return read


def main_kernel(count, cut, perm_ref, up_a, gate_a, down_a, up_b, gate_b, down_b, *refs):
    begin_ref, means, costs_ref, refs = refs[0], refs[1:4], refs[4], refs[5:]
    sent, moved, refs = refs[:4], refs[4:8], refs[8:]
    hot, halves, padded, slot, table, begins, ask, got, asked, held, window, windows, wide, rows, spread, turn, stage = refs[:17]
    part, shares, refs = refs[17], refs[18], refs[19:]
    ask_send, ask_recv, win_send, win_recv, item_send, item_recv, share_send, share_recv, strip_sems, load_sems, stage_sems, own_sem = refs
    me, column = lax.axis_index("rows"), lax.axis_index("cols")
    slots = count // PEERS
    stride = count // A_DEV
    cols = part.shape[0]
    features = up_a.shape[1]
    widths = (features, features, cut, features - cut)
    barrier = pltpu.get_barrier_semaphore()
    for k in range(1, PEERS):
        pl.semaphore_signal(barrier, inc=1, device_id={"rows": me ^ k}, device_id_type=MESH)
    for k in range(1, cols):
        pl.semaphore_signal(barrier, inc=1, device_id={"cols": column ^ k}, device_id_type=MESH)

    strips = []
    for m, ref in enumerate((up_a, gate_a)):
        for i in range(A_DEV):
            at = m * A_DEV + i
            strips.append(
                pltpu.make_async_copy(ref.at[pl.ds(i * stride, 16)], held.at[pl.ds(at * 16, 16)], strip_sems.at[at])
            )
    for copy in strips:
        copy.start()
    loads = [
        pltpu.make_async_copy(up_b, rows, load_sems.at[0]),
        pltpu.make_async_copy(gate_b, means[1], load_sems.at[1]),
    ]
    for copy in loads:
        copy.start()

    def remote(src, dst, send, recv, peer, axis="rows"):
        return pltpu.make_async_remote_copy(
            src_ref=src, dst_ref=dst, send_sem=send, recv_sem=recv, device_id={axis: peer}, device_id_type=MESH
        )

    count_ranks(count, me, perm_ref, slot, hot, halves, padded, ask)
    pl.semaphore_wait(barrier, PEERS - 1 + cols - 1)
    asks = [remote(ask.at[me ^ k], got.at[k], ask_send.at[k], ask_recv.at[k], me ^ k) for k in ORDER]
    for copy in asks:
        copy.start()
    own = pltpu.make_async_copy(ask.at[me], got.at[0], own_sem)
    own.start()
    for copy in strips:
        copy.wait()
    shape = (2 * A_DEV, 32 * A_DEV)
    first = lax.broadcasted_iota(jnp.int32, shape, 0) * 16 == lax.broadcasted_iota(jnp.int32, shape, 1)
    window[...] = matmul(one_hot(first), held[...]).astype(jnp.bfloat16)
    windows[0] = window[...]
    across = [remote(window, windows.at[k], win_send.at[k], win_recv.at[k], me ^ k) for k in (6, 2, 4)]
    for copy in across:
        copy.start()

    begin_ref[...] = first_of(slot[...], widths[3] // LANES)
    loads[0].wait()
    spread_out(rows, spread)
    own.wait()
    for copy in asks:
        copy.wait()
    got[...] = first_of(jnp.clip(got[...], 0, count - 1), features // LANES)
    own = pltpu.make_async_copy(got, asked, own_sem)
    own.start()
    own.wait()

    def gather(k, buffer):
        def step(t, carry):
            for row, c, tile in rows_of(lambda s: asked[k, 0, t * ROWS + s], spread, turn, features // LANES):
                at = pl.ds(pl.multiple_of(t * ROWS + row, 16), 16)
                stage[buffer, at, c * LANES : (c + 1) * LANES] = tile.astype(jnp.bfloat16)
            return carry

        lax.fori_loop(0, slots // ROWS, step, 0)

    items = [(a, k) for a in range(4) for k in (ORDER if a < 2 else LATER)]

    def item(a, k):
        return remote(sent[a].at[k], moved[a].at[k], item_send.at[a, k], item_recv.at[a, k], me ^ k)

    def up_step(n, carry):
        k = n ^ 6
        gather(k, 0)
        copy = pltpu.make_async_copy(stage.at[0], sent[0].at[k], stage_sems.at[0])
        copy.start()
        copy.wait()

        @pl.when(k > 0)
        def _():
            item(0, k).start()

        return carry

    lax.fori_loop(0, PEERS, up_step, 0)
    done = {"sent": len(ORDER), "here": 0}

    def push(count_of):
        while done["sent"] < count_of:
            item(*items[done["sent"]]).start()
            done["sent"] += 1

    def receive(until, last=None):
        while done["here"] < until:
            item(*items[done["here"]]).wait_recv()
            done["here"] += 1
            push(min(done["here"] + AHEAD, last or len(items)))

    for copy in across:
        copy.wait()
    beside = [remote(windows.at[k], windows.at[k + 1], win_send.at[k + 1], win_recv.at[k + 1], me ^ 1) for k in (0, 2, 4, 6)]
    for copy in beside:
        copy.start()

    def collect(*arrays):
        def copies(k, buffer):
            begin = 0
            for n, a in enumerate(arrays):
                src = stage.at[buffer, :, pl.ds(begin, widths[a])]
                begin += widths[a]
                yield pltpu.make_async_copy(src, sent[a].at[k], stage_sems.at[2 * n + buffer])

        def step(n, carry):
            buffer = n & 1

            @pl.when(n >= 2)
            def _():
                for copy in copies(0, buffer):
                    copy.wait()

            gather(n ^ 6, buffer)
            for copy in copies(n ^ 6, buffer):
                copy.start()
            return carry

        lax.fori_loop(0, PEERS, step, 0)
        for buffer in range(2):
            for copy in copies(0, buffer):
                copy.wait()

    loads[1].wait()
    spread_out(means[1], spread)
    collect(1)
    push(AHEAD)

    for copy in beside:
        copy.wait()
    for k in range(PEERS):
        for m in range(2):
            wide[m, k * A_DEV : (k + 1) * A_DEV, :] = windows[k, m * A_DEV : (m + 1) * A_DEV, :]
    group = part.shape[2]

    def cost(j, carry):
        at = pl.ds(pl.multiple_of(j * COST_ROWS, COST_ROWS), COST_ROWS)
        both = [
            lax.dot_general(wide[m], ref[at, :], OVER_LANES, preferred_element_type=jnp.float32)
            for m, ref in enumerate((rows, means[1]))
        ]
        value = both[0] + both[1]
        for k in range(PEERS):
            for c in range(cols):
                begin = k * A_DEV + c * group
                part[c, me ^ k, :, at] = value[begin : begin + group]
        return carry

    lax.fori_loop(0, count // COST_ROWS, cost, 0)
    exchanged = [
        remote(part.at[column ^ k], shares.at[k - 1], share_send.at[k], share_recv.at[k], column ^ k, "cols")
        for k in range(1, cols)
    ]
    for copy in exchanged:
        copy.start()
    load = pltpu.make_async_copy(down_b, rows, load_sems.at[0])
    load.start()
    load.wait()
    spread_out(rows, spread)
    collect(2, 3)

    def place(a, initial):
        width, out = widths[a], means[a]
        tiles = width // LANES
        lanes = pl.ds(0, width)
        table[...] = first_of(slot[...], tiles)
        to_table = pltpu.make_async_copy(table, begins, own_sem)
        to_table.start()
        ours = pltpu.make_async_copy(initial.at[:, lanes], out, load_sems.at[1])
        ours.start()
        own_rows = pltpu.make_async_copy(sent[a].at[0], rows.at[pl.ds(0, slots), lanes], stage_sems.at[0])
        own_rows.start()
        fetched = [
            pltpu.make_async_copy(moved[a].at[k], rows.at[pl.ds(k * slots, slots), lanes], strip_sems.at[k])
            for k in range(1, PEERS)
        ]
        for copy in fetched:
            copy.start()
        own_rows.wait()
        for copy in fetched:
            copy.wait()
        spread_out(rows, spread, tiles)
        to_table.wait()
        ours.wait()
        read = table_reader(begins)

        def step(j, carry):
            for row, c, tile in rows_of(lambda s: read(j, s), spread, turn, tiles):
                at = pl.ds(pl.multiple_of(j * ROWS + row, 16), 16)
                columns = slice(c * LANES, (c + 1) * LANES)
                out[at, columns] = ((out[at, columns].astype(jnp.float32) + tile) * 0.5).astype(jnp.bfloat16)
            return carry

        lax.fori_loop(0, count // ROWS, step, 0)

    held_back = 3 * len(ORDER)
    receive(len(ORDER), held_back)
    place(0, up_a)
    receive(2 * len(ORDER), held_back)
    place(1, gate_a)
    for copy in exchanged:
        copy.wait()
    for block in range(PEERS):
        value = part[column, block]
        for k in range(1, cols):
            value = value + shares[k - 1, block]
        value = value * (2.0 * D) ** (-0.5)
        for m in range(group):
            costs_ref[m * PEERS + block : m * PEERS + block + 1, :] = value[m : m + 1]
    receive(held_back - 3, held_back)
    push(len(items))
    receive(held_back)
    place(2, down_a)
    receive(len(items))
    for a, k in items:
        item(a, k).wait_send()


def last_kernel(cut, begin_ref, up_ref, gate_ref, down_ref, costs_ref, own_ref, moved_ref, initial, *refs):
    up_out, gate_out, down_out, costs_out, table, begins, rows, ours, spread, turn, sems, out_sems = refs
    count, features = initial.shape
    slots = count // PEERS
    width = features - cut
    tiles = width // LANES
    left, right = pl.ds(0, cut), pl.ds(cut, width)
    fetched = [pltpu.make_async_copy(own_ref.at[0], rows.at[pl.ds(0, slots)], sems.at[0])]
    fetched += [
        pltpu.make_async_copy(moved_ref.at[k], rows.at[pl.ds(k * slots, slots)], sems.at[k]) for k in range(1, PEERS)
    ]
    fetched.append(pltpu.make_async_copy(initial.at[:, right], ours, sems.at[PEERS]))
    table[...] = paired(begin_ref[...])
    fetched.append(pltpu.make_async_copy(table, begins, sems.at[PEERS + 1]))
    ways = ((up_ref, up_out), (gate_ref, gate_out), (down_ref, down_out.at[:, left]), (costs_ref, costs_out))
    handed = [pltpu.make_async_copy(src, dst, out_sems.at[n]) for n, (src, dst) in enumerate(ways)]
    for copy in fetched:
        copy.start()
    for copy in fetched:
        copy.wait()
    for copy in handed:
        copy.start()
    spread_out(rows, spread)
    read = table_reader(begins)

    def step(j, carry):
        for row, c, tile in rows_of(lambda s: half(lambda even: read(j, even), s), spread, turn, tiles):
            at = pl.ds(pl.multiple_of(j * ROWS + row, 16), 16)
            columns = slice(c * LANES, (c + 1) * LANES)
            ours[at, columns] = ((ours[at, columns].astype(jnp.float32) + tile) * 0.5).astype(jnp.bfloat16)
        return carry

    piece = count // PARTS
    steps = piece // ROWS
    written = []
    for n in range(PARTS):
        lax.fori_loop(n * steps, (n + 1) * steps, step, 0)
        at = pl.ds(n * piece, piece)
        written.append(pltpu.make_async_copy(ours.at[at], down_out.at[at, right], sems.at[n]))
        written[n].start()
    for copy in handed + written:
        copy.wait()


def balanced(up_a, gate_a, down_a, up_b, gate_b, down_b, perm):
    count, features = up_a.shape
    cols = lax.axis_size("cols")
    cut = features * 3 // 4
    used = count // LANES
    pad = -(-used // 8) * 8
    slots = count // PEERS
    lanes = -(-slots // LANES) * LANES
    tiles = features // LANES
    vmem, hbm = pl.BlockSpec(memory_space=pltpu.VMEM), pl.BlockSpec(memory_space=pltpu.HBM)
    bf16, f32, i32 = jnp.bfloat16, jnp.float32, jnp.int32
    group = A_DEV // cols
    whole, kept = jax.ShapeDtypeStruct((count, features), bf16), pltpu.VMEM((count, features), bf16)
    costs_shape = jax.ShapeDtypeStruct((group * PEERS, count), f32)
    lists = [jax.ShapeDtypeStruct((PEERS, slots, size), bf16) for size in (features, features, cut, features - cut)]
    begins, *parts = pl.pallas_call(
        functools.partial(main_kernel, count, cut),
        out_shape=[pltpu.VMEM((pad, LANES), i32), kept, kept, pltpu.VMEM((count, cut), bf16), pltpu.VMEM(costs_shape.shape, f32)]
        + lists * 2,
        in_specs=[vmem] + [hbm] * 6,
        out_specs=[vmem] * 5 + [hbm] * 8,
        scratch_shapes=[
            pltpu.VMEM((slots, count), bf16),
            pltpu.VMEM((2 * PEERS, count), bf16),
            pltpu.VMEM((pad, LANES), i32),
            pltpu.VMEM((pad, LANES), i32),
            pltpu.VMEM((pad, LANES), i32),
            pltpu.SMEM((pad, LANES), i32),
            pltpu.VMEM((PEERS, 8, lanes), i32),
            pltpu.VMEM((PEERS, 8, lanes), i32),
            pltpu.SMEM((PEERS, 8, lanes), i32),
            pltpu.VMEM((32 * A_DEV, features), bf16),
            pltpu.VMEM((2 * A_DEV, features), bf16),
            pltpu.VMEM((PEERS, 2 * A_DEV, features), bf16),
            pltpu.VMEM((2, A_DEV * PEERS, features), bf16),
            pltpu.VMEM((count, features), bf16),
            pltpu.VMEM(((count + 8) * tiles, LANES), f32),
            pltpu.VMEM(((ROWS + 8) * tiles, LANES), f32),
            pltpu.VMEM((2, slots, features), bf16),
            pltpu.VMEM((cols, PEERS, group, count), f32),
            pltpu.VMEM((cols - 1, PEERS, group, count), f32),
        ]
        + [pltpu.SemaphoreType.DMA((PEERS,))] * 4
        + [pltpu.SemaphoreType.DMA((4, PEERS))] * 2
        + [pltpu.SemaphoreType.DMA((cols,))] * 2
        + [
            pltpu.SemaphoreType.DMA((2 * A_DEV,)),
            pltpu.SemaphoreType.DMA((2,)),
            pltpu.SemaphoreType.DMA((4,)),
            pltpu.SemaphoreType.DMA,
        ],
        compiler_params=pltpu.CompilerParams(
            collective_id=0, has_side_effects=True, vmem_limit_bytes=40 * 1024 * 1024
        ),
    )(perm.reshape(used, LANES), up_a, gate_a, down_a, up_b, gate_b, down_b)
    near = [pltpu.with_memory_space_constraint(part, pltpu.VMEM) for part in (begins, *parts[:4])]
    own, moved, initial = (pltpu.with_memory_space_constraint(part, pltpu.HBM) for part in (parts[7], parts[11], down_a))
    width = features - cut
    up_mean, gate_mean, down_mean, costs = pl.pallas_call(
        functools.partial(last_kernel, cut),
        out_shape=[whole, whole, whole, costs_shape],
        in_specs=[vmem] * 5 + [hbm] * 3,
        out_specs=[hbm] * 4,
        scratch_shapes=[
            pltpu.VMEM((pad, LANES), i32),
            pltpu.SMEM((pad, LANES), i32),
            pltpu.VMEM((count, width), bf16),
            pltpu.VMEM((count, width), bf16),
            pltpu.VMEM(((count + 8) * width // LANES, LANES), f32),
            pltpu.VMEM(((ROWS + 8) * width // LANES, LANES), f32),
            pltpu.SemaphoreType.DMA((PEERS + 2,)),
            pltpu.SemaphoreType.DMA((4,)),
        ],
        compiler_params=pltpu.CompilerParams(vmem_limit_bytes=12 * 1024 * 1024),
    )(*near, own, moved, initial)
    return (costs.T, up_mean, gate_mean, down_mean)


def pick(array, index):
    rows = jnp.arange(array.shape[0], dtype=jnp.int32)
    hot = (index[:, None] == rows[None, :]).astype(array.dtype)
    return jnp.dot(hot, array, preferred_element_type=jnp.float32).astype(array.dtype)


def mix(initial, picked):
    return ((initial.astype(jnp.float32) + picked.astype(jnp.float32)) * 0.5).astype(jnp.bfloat16)


def general(up_a, gate_a, down_a, up_b, gate_b, down_b, perm):
    row_count, features = up_a.shape
    stride = row_count // A_DEV
    cost_scale = (2.0 * D) ** (-0.5)
    peers = lax.axis_size("rows")
    cols = lax.axis_size("cols")
    capacity = max(2, (row_count + peers - 1) // peers)

    source = perm // row_count
    local_row = perm % row_count
    blocks = jnp.arange(peers, dtype=jnp.int32)
    matches = (source[None, :] == blocks[:, None]).astype(jnp.int32)
    order = jnp.arange(row_count, dtype=jnp.int32)
    ahead = jnp.dot(
        matches.astype(jnp.bfloat16),
        (order[:, None] < order[None, :]).astype(jnp.bfloat16),
        preferred_element_type=jnp.float32,
    )
    arrival_rank = jnp.sum(ahead.astype(jnp.int32) * matches, axis=0)
    high = (local_row // 256).astype(jnp.bfloat16)
    low = (local_row % 256).astype(jnp.bfloat16)
    halves = jnp.stack([high, low])[:, None, :] * matches.astype(jnp.bfloat16)[None]
    at_rank = (arrival_rank[None, :] == jnp.arange(capacity, dtype=jnp.int32)[:, None]).astype(jnp.bfloat16)
    found = jnp.einsum("hsi,ri->hsr", halves, at_rank, preferred_element_type=jnp.float32)
    wanted = found[0].astype(jnp.int32) * 256 + found[1].astype(jnp.int32)
    asked = lax.all_to_all(wanted, "rows", split_axis=0, concat_axis=0, tiled=True).reshape(-1)
    slot = source * capacity + arrival_rank

    window = jnp.concatenate([up_a[::stride], gate_a[::stride]], axis=0)
    pieces = lax.all_gather(window, "rows").reshape(peers, 2, A_DEV, features)
    wide = pieces.transpose(1, 2, 0, 3).reshape(2, A_DEV * peers, features)
    partial_value = jnp.einsum("kd,jd->kj", wide[0], up_b, preferred_element_type=jnp.float32)
    partial_value = partial_value + jnp.einsum("kd,jd->kj", wide[1], gate_b, preferred_element_type=jnp.float32)
    total = lax.psum_scatter(partial_value.reshape(cols, -1, row_count), "cols", scatter_dimension=0)

    def averaged(initial, other):
        moved = pick(other, asked).reshape(peers, capacity, features)
        moved = lax.all_to_all(moved, "rows", split_axis=0, concat_axis=0, tiled=True)
        return mix(initial, pick(moved.reshape(-1, features), slot))

    return (
        (total * cost_scale).T,
        averaged(up_a, up_b),
        averaged(gate_a, gate_b),
        averaged(down_a, down_b),
    )


def solution(mesh):
    def local(up_a, *rest):
        row_count, features = up_a.shape
        even = mesh.shape["rows"] == PEERS and row_count % (PEERS * 16) == 0 and row_count % (A_DEV * 16) == 0
        even = even and row_count % COST_ROWS == 0 and row_count % (ROWS * PARTS) == 0 and row_count % (PEERS * ROWS) == 0
        even = even and features == 8 * LANES and mesh.shape["cols"] == A_DEV // 8 and row_count * 8 < 2**15
        return (balanced if even else general)(up_a, *rest)

    placed = (P("rows", "cols"),) * 6 + (P("rows"),)
    return jax.shard_map(
        local,
        mesh=mesh,
        in_specs=placed,
        out_specs=(P("rows", "cols"),) * 4,
        check_vma=False,
    )
```
